32 devices in a mesh: expert: 8 (over z, x), chan: 4 (over y, core).
Axes of the slice: x: 2, y: 2, z: 4, core: 2. Of those that a mesh axis runs over, the one named last changes fastest.
Arguments:
- rows_in: bfloat16 [256, 6144], P('expert', 'chan'), may hold values from -6 to 6
- expert_picks: int32 [256, 2], P('expert'), may hold values from 0 to 3, all different within a row; in each aligned block of 32 rows (0 to 31, 32 to 63, ...) at most 18 rows name the same one
- latent_ids: int32 [256, 2, 32], P('expert'), may hold values from 0 to 8191, as said below
- enc_weight: bfloat16 [6144, 32768], P('chan', 'expert'), may hold values from -0.078125 to 0.078125
- dec_weight: bfloat16 [32768, 6144], P('expert', 'chan'), may hold values from -0.375 to 0.375
Outputs:
- recon_error: bfloat16 [256, 6144], P('expert', 'chan')
- enc_grad: float32 [6144, 32768], P('chan', 'expert')
- dec_grad: float32 [32768, 6144], P('expert', 'chan')
The draws below stay inside these ranges and needn't reach their ends.
Inputs may be any that keep to these rules, and one draw needn't show every extreme that they name: `expert_picks`: A row's two experts differ; among the 32 rows of one device at most 18 name one expert. latent_ids[r, j, k] lies in k * 256 to (k + 1) * 256 - 1 and numbers a latent of expert expert_picks[r, j].
All inputs are finite; a program needn't handle non-finite values.
Results may differ from the reference program's by a relative error of at most 0.0095.
Values may be sent and summed in bfloat16 or wider, within the bound.
No kernel may reach another device: no remote copies, remote signals or barrier semaphores. Data moves between devices by JAX's collectives and lax.ppermute only.
A program may use at most 128 MiB of HBM per device.

```python
import math
import jax
import jax.numpy as jnp
import numpy as np

C = 6144
LAT = 8192
EXPERTS = 4
TOPK = 32
ROW_DEV = 32
CAP = 18
ROWS = 256
LAT_ALL = 32768


def draw_latent_ids(key, part):
    stride = LAT // TOPK
    offsets = jax.random.randint(key, (ROWS, 2, TOPK), 0, stride, dtype=jnp.int32)
    starts = jnp.arange(TOPK, dtype=jnp.int32) * stride
    return offsets + starts[None, None, :]


def shard_levels(stream_key, extent, split, low, top_value):
    gain, own = 1.0, jax.random.fold_in(stream_key, 6)
    for dim, parts in split:
        steps = jnp.exp(jax.random.uniform(jax.random.fold_in(own, dim), (parts,), jnp.float32, low / len(split), top_value / len(split)))
        gain = gain * jnp.repeat(steps, extent[dim] // parts).reshape([-1 if axis == dim else 1 for axis in range(len(extent))])
    return gain


def assign_block(own_key, own, number, rows, amount, top, most, slope):
    order = jax.random.permutation(own_key, amount)
    heavy_load, ordinary = portions_of(amount, rows * top, most, slope, True), portions_of(amount, rows * top, most, slope, False)
    places = jnp.arange(amount)

    def named(sizes, offset_by):
        used = int((sizes > 0).sum())
        fixed = max(1, used // 4)
        moved = fixed + (places - fixed + offset_by * (used - fixed)) % max(1, amount - fixed)
        return jnp.zeros((amount,), jnp.int32).at[order[jnp.where(places < fixed, places, moved)]].set(jnp.asarray(sizes, jnp.int32))

    sizes = jnp.where(number % 4 == 0, named(heavy_load, number // 4), named(ordinary, number - number // 4 - 1))
    mixed = jax.random.permutation(jax.random.fold_in(own, 3), amount)
    giver, receiver = mixed[0:amount // 2 * 2:2], mixed[1:amount // 2 * 2:2]
    slack = jnp.minimum(sizes[giver] - 1, most - sizes[receiver]) // 2
    slack = jnp.where((giver == order[0]) | (receiver == order[0]) | (sizes[receiver] == 0), 0, jnp.maximum(slack, 0))
    moved = jax.random.randint(jax.random.fold_in(own, 4), (amount // 2,), 0, 1 << 20) % (slack + 1)
    sizes = sizes.at[giver].add(-moved).at[receiver].add(moved)
    labels = jnp.searchsorted(jnp.cumsum(sizes), jnp.arange(rows * top), side="right").astype(jnp.int32)
    table = labels.reshape(top, rows).T
    table = table[jax.random.permutation(jax.random.fold_in(own, 1), rows)]
    offset_by = jax.random.randint(jax.random.fold_in(own, 2), (rows, 1), 0, top)
    return jnp.take_along_axis(table, (jnp.arange(top)[None, :] + offset_by) % top, axis=1)


def portions_of(number_of, total, limit, lean, full):
    weights = [(1 << 20) // math.isqrt(rank ** lean) + 1 for rank in range(1, number_of + 1)]
    largest = limit if full else min(limit, max(-(-total // number_of), total * weights[0] // sum(weights)))
    least = 1 if total - largest >= number_of - 1 else 0
    given, rest = [largest] + [least] * (number_of - 1), total - largest - least * (number_of - 1)
    while rest > 0:
        candidates = [i for i in range(1, number_of) if given[i] < largest] or [i for i in range(1, number_of) if given[i] < limit]
        mass, left = sum([weights[i] for i in candidates]), rest
        for i in candidates:
            addition = min(limit - given[i], max(1, left * weights[i] // mass), rest)
            given[i] = given[i] + addition
            rest = rest - addition
    return np.array(given)


def centred(stream_key, extent, deviation, reach, split=(), kind=jnp.bfloat16):
    gain = shard_levels(stream_key, extent, split, -0.22, 0.18) if split else 1.0
    result = jax.random.normal(stream_key, extent, jnp.float32) * deviation * gain
    return jnp.minimum(jnp.maximum(result, -reach), reach).astype(kind)


def setup_inputs(seed: int = 0) -> dict:
    key_list = jax.random.split(jax.random.key(seed), 6)
    rows_in = centred(key_list[0], (ROWS, C), 1.0, 6.0, ((0, 8), (1, 4)))
    expert_picks_keys = jax.random.split(jax.random.fold_in(key_list[1], 1), ROWS // ROW_DEV)
    expert_picks_turns = jax.random.permutation(jax.random.fold_in(key_list[1], 3), ROWS // ROW_DEV)
    expert_picks = jax.vmap(lambda own, number: assign_block(jax.random.fold_in(key_list[1], 2), own, number, ROW_DEV, EXPERTS, 2, CAP, 2))(expert_picks_keys, expert_picks_turns).reshape((ROWS, 2))
    latent_ids = draw_latent_ids(jax.random.fold_in(key_list[5], 71), 0)
    enc_weight = centred(key_list[3], (C, LAT_ALL), C ** -0.5, 0.078125, ((0, 4), (1, 8)))
    dec_weight = centred(key_list[4], (LAT_ALL, C), (8 * TOPK) ** -0.5, 0.375, ((0, 8), (1, 4)))
    return dict(rows_in=rows_in, expert_picks=expert_picks, latent_ids=latent_ids, enc_weight=enc_weight, dec_weight=dec_weight)


def expert_parts(rows_in, expert_picks, latent_ids, enc_weight, dec_weight, expert_id):
    stride = LAT // TOPK
    hit_table = (expert_picks == expert_id).astype(jnp.int32)
    chosen = jnp.sum(hit_table[:, :, None] * (latent_ids + 1), axis=1) - 1
    spread = jnp.repeat(chosen, stride, axis=1)
    live_mask = spread == jnp.arange(LAT, dtype=jnp.int32)[None, :]
    enc_part = enc_weight[:, expert_id * LAT:(expert_id + 1) * LAT]
    dec_part = dec_weight[expert_id * LAT:(expert_id + 1) * LAT, :]
    preact = jnp.dot(rows_in, enc_part, preferred_element_type=jnp.float32)
    activation = jnp.where(live_mask, preact, jnp.float32(0.0)).astype(jnp.bfloat16)
    return live_mask, activation, dec_part


def reference(rows_in, expert_picks, latent_ids, enc_weight, dec_weight):
    recon = jnp.zeros((rows_in.shape[0], rows_in.shape[1]), jnp.float32)
    for expert_id in range(EXPERTS):
        live_mask, activation, dec_part = expert_parts(rows_in, expert_picks, latent_ids, enc_weight, dec_weight, expert_id)
        recon = recon + jnp.dot(activation, dec_part, preferred_element_type=jnp.float32)
    recon_error = (recon - rows_in.astype(jnp.float32)).astype(jnp.bfloat16)
    enc_parts = []
    dec_parts = []
    for expert_id in range(EXPERTS):
        live_mask, activation, dec_part = expert_parts(rows_in, expert_picks, latent_ids, enc_weight, dec_weight, expert_id)
        act_grad = jnp.dot(recon_error, dec_part.T, preferred_element_type=jnp.float32)
        pre_grad = jnp.where(live_mask, act_grad, jnp.float32(0.0)).astype(jnp.bfloat16)
        dec_parts.append(jnp.dot(activation.T, recon_error, preferred_element_type=jnp.float32))
        enc_parts.append(jnp.dot(rows_in.T, pre_grad, preferred_element_type=jnp.float32))
    return recon_error, jnp.concatenate(enc_parts, axis=1), jnp.concatenate(dec_parts, axis=0)
```

```python
import jax
import jax.numpy as jnp
from jax import lax
from jax.sharding import PartitionSpec as P

LAT = 8192
EXPERTS = 4
TOPK = 32
CAP = 18


def spread(values, places, stride):
    ids = lax.iota(jnp.int32, stride)
    hit = places[:, :, None] == ids[None, None, :]
    table = jnp.where(hit, values[:, :, None], 0.0).astype(jnp.bfloat16)
    return table.reshape(values.shape[0], values.shape[1] * stride)


def gather_live(partial, places, stride):
    ids = lax.iota(jnp.int32, stride)
    hit = places[:, :, None] == ids[None, None, :]
    return jnp.sum(jnp.where(hit, partial.reshape(hit.shape), 0.0), axis=2)


def live_places(chosen, lat_low, lat_local):
    stride = LAT // TOPK
    first = lat_low // stride
    count = lat_local // stride
    id_block = lax.dynamic_slice_in_dim(chosen, first, count, 1)
    return id_block - (first + lax.iota(jnp.int32, count))[None, :] * stride


def encode(flat_rows, places, enc_weight):
    stride = LAT // TOPK
    partial_pre = jnp.dot(flat_rows, enc_weight, preferred_element_type=jnp.float32)
    live = lax.psum(gather_live(partial_pre, places, stride), "chan")
    return spread(live, places, stride)


def gradients(flat_rows, flat_errors, places, activation, dec_weight):
    stride = LAT // TOPK
    partial_grad = lax.dot_general(
        flat_errors, dec_weight, (((1,), (1,)), ((), ())), preferred_element_type=jnp.float32
    )
    live = lax.psum(gather_live(partial_grad, places, stride), "chan")
    pre_grad = spread(live, places, stride)
    dec_grad = lax.dot_general(
        activation, flat_errors, (((0,), (0,)), ((), ())), preferred_element_type=jnp.float32
    )
    enc_grad = lax.dot_general(
        flat_rows, pre_grad, (((0,), (0,)), ((), ())), preferred_element_type=jnp.float32
    )
    return (enc_grad, dec_grad)


def per_device(rows_in, expert_picks, latent_ids, enc_weight, dec_weight):
    row_count, chan_width = rows_in.shape
    devices = lax.axis_size("expert")
    group_size = devices // EXPERTS
    lat_local = enc_weight.shape[1]
    position = lax.axis_index("expert")
    lat_low = position % group_size * lat_local
    capacity = CAP
    hit_table = (expert_picks[:, :, None] == lax.iota(jnp.int32, EXPERTS)[None, None, :]).astype(
        jnp.int32
    )
    member = jnp.sum(hit_table, axis=1)
    earlier = (
        lax.iota(jnp.int32, row_count)[None, :] < lax.iota(jnp.int32, row_count)[:, None]
    ).astype(jnp.int32)
    slot_index = jnp.dot(earlier, member)
    slot_table = (slot_index[:, :, None] == lax.iota(jnp.int32, capacity)[None, None, :]) & (
        member[:, :, None] > 0
    )
    slot_bf = slot_table.astype(jnp.bfloat16)
    picked_ids = jnp.einsum("rje,rjk->rek", hit_table, latent_ids + 1)
    sent_rows = jnp.einsum(
        "rec,rd->ecd", slot_bf, rows_in, preferred_element_type=jnp.float32
    ).astype(jnp.bfloat16)
    sent_ids = jnp.einsum("rec,rek->eck", slot_table.astype(jnp.int32), picked_ids) - 1

    def fan_out(table):
        wide = jnp.broadcast_to(table[:, None], (EXPERTS, group_size) + table.shape[1:])
        return wide.reshape((devices,) + table.shape[1:])

    got_rows, got_ids = (
        lax.all_to_all(fan_out(sent_rows), "expert", split_axis=0, concat_axis=0, tiled=True),
        lax.all_to_all(fan_out(sent_ids), "expert", split_axis=0, concat_axis=0, tiled=True),
    )
    flat_rows = got_rows.reshape(devices * capacity, chan_width)
    chosen = got_ids.reshape(devices * capacity, TOPK)
    places = live_places(chosen, lat_low, lat_local)
    activation = encode(flat_rows, places, enc_weight)
    partial_recon = jnp.dot(activation, dec_weight, preferred_element_type=jnp.float32)
    returned = lax.all_to_all(
        partial_recon.reshape(devices, capacity, chan_width).astype(jnp.bfloat16),
        "expert",
        split_axis=0,
        concat_axis=0,
        tiled=True,
    ).astype(jnp.float32)
    per_expert = jnp.sum(returned.reshape(EXPERTS, group_size, capacity, chan_width), axis=1)
    recon = jnp.einsum(
        "rec,ecd->rd", slot_table.astype(jnp.float32), per_expert, precision=lax.Precision.HIGHEST
    )
    recon_error = (recon - rows_in.astype(jnp.float32)).astype(jnp.bfloat16)
    sent_errors = jnp.einsum(
        "rec,rd->ecd", slot_bf, recon_error, preferred_element_type=jnp.float32
    ).astype(jnp.bfloat16)
    got_errors = lax.all_to_all(
        fan_out(sent_errors), "expert", split_axis=0, concat_axis=0, tiled=True
    )
    flat_errors = got_errors.reshape(devices * capacity, chan_width)
    enc_grad, dec_grad = gradients(flat_rows, flat_errors, places, activation, dec_weight)
    return (recon_error, enc_grad, dec_grad)


def solution(mesh):
    placed = (
        P("expert", "chan"),
        P("expert", None),
        P("expert", None, None),
        P("chan", "expert"),
        P("expert", "chan"),
    )
    return jax.shard_map(
        per_device,
        mesh=mesh,
        in_specs=placed,
        out_specs=(P("expert", "chan"), P("chan", "expert"), P("expert", "chan")),
        check_vma=False,
    )
```

```python
import functools

import jax
import jax.numpy as jnp
from jax import lax
from jax.experimental import pallas as pl
from jax.experimental.pallas import tpu as pltpu
from jax.sharding import PartitionSpec as P

LAT = 8192
EXPERTS = 4
TOPK = 32
CAP = 18
STRIDE = LAT // TOPK
LANES = 128
F32 = jnp.float32
BF16 = jnp.bfloat16
PARAMS = pltpu.CompilerParams(vmem_limit_bytes=40 * 1024 * 1024)


def up(value, step):
    return -(-value // step) * step


def iota(shape, dim):
    return lax.broadcasted_iota(jnp.int32, shape, dim)


def dot(left, right, dims):
    return lax.dot_general(left, right, (dims, ((), ())), preferred_element_type=F32)


NN = ((1,), (0,))
NT = ((1,), (1,))
TN = ((0,), (0,))


def put_slots(message_ref, device, table, first):
    for piece in range(table.shape[1] // LANES):
        message_ref[device, pl.ds((first + piece) * CAP, CAP), :] = table[
            :, piece * LANES : (piece + 1) * LANES
        ]


def take_slots(message_ref, device, flat_ref, row):
    for piece in range(flat_ref.shape[1] // LANES):
        flat_ref[pl.ds(row, CAP), piece * LANES : (piece + 1) * LANES] = message_ref[
            device, pl.ds(piece * CAP, CAP), :
        ]


def clear(flat_ref, first):
    if first < flat_ref.shape[0]:
        shape = (flat_ref.shape[0] - first, flat_ref.shape[1])
        flat_ref[first:, :] = jnp.zeros(shape, BF16)


def dispatch_kernel(group, blocks, picks_ref, ids_ref, rows_ref, slots_ref, message_ref):
    rows = rows_ref.shape[0]
    shape = (EXPERTS * CAP, rows)
    number = iota(shape, 0)
    expert = sum((number >= CAP * e).astype(jnp.int32) for e in range(1, EXPERTS))
    place = number - expert * CAP
    hits = [picks_ref[j : j + 1, :] == expert for j in range(2)]
    member = (hits[0] | hits[1]).astype(BF16)
    earlier = (iota((rows, rows), 0) < iota((rows, rows), 1)).astype(BF16)
    slot = dot(member, earlier, NN)
    here = slot == place.astype(F32)
    chosen = [(hit & here).astype(BF16) for hit in hits]
    slots = chosen[0] + chosen[1]
    slots_ref[...] = slots
    sent = dot(slots, rows_ref[...], NN).astype(BF16)
    first = iota((rows, TOPK), 1) * STRIDE
    sent_places = sum(
        dot(chosen[j], (ids_ref[:, j, :] - first + 1).astype(BF16), NN) for j in range(2)
    )
    sent_places = (sent_places - 1.0).astype(BF16)
    pieces = rows_ref.shape[1] // LANES
    empty = jnp.full((CAP, LANES), -1.0, BF16)
    for device in range(message_ref.shape[0]):
        e, low = device // group, device % group * blocks
        part = slice(e * CAP, (e + 1) * CAP)
        put_slots(message_ref, device, sent[part], 0)
        message_ref[device, pl.ds(pieces * CAP, CAP), :] = empty
        message_ref[device, pl.ds(pieces * CAP, CAP), 0:blocks] = sent_places[
            part, low : low + blocks
        ]


def encode_kernel(
    devices, message_ref, enc_ref, rows_t_ref, places_ref, places_t_ref, live_ref, flat, wide, live
):
    blocks = enc_ref.shape[1] // STRIDE
    slots = devices * CAP
    pieces = flat.shape[1] // LANES
    step = pl.program_id(0)

    @pl.when(step == 0)
    def _():
        wide[...] = jnp.full(wide.shape, -1.0, F32)
        live[...] = jnp.zeros(live.shape, F32)
        for device in range(devices):
            take_slots(message_ref, device, flat, device * CAP)
            wide[pl.ds(device * CAP, CAP), :] = message_ref[
                device, pl.ds(pieces * CAP, CAP), :
            ].astype(F32)
        places_ref[...] = wide[...]

    partial = dot(flat[0:slots, :], enc_ref[...], NN)
    lane = iota((slots, STRIDE), 1).astype(F32)
    column = iota((slots, LANES), 1)
    for block in range(blocks):
        index = step * blocks + block
        place = jnp.sum(
            jnp.where(column == index, wide[0:slots, :], 0.0), axis=1, keepdims=True
        )
        part = partial[:, block * STRIDE : (block + 1) * STRIDE]
        value = jnp.sum(jnp.where(place == lane, part, 0.0), axis=1, keepdims=True)
        live[0:slots, :] = jnp.where(column == index, value, live[0:slots, :])

    @pl.when(step == pl.num_programs(0) - 1)
    def _():
        count = live_ref.shape[0]
        live_ref[...] = live[...].T[0:count, :]
        places_t_ref[...] = wide[...].T[0:count, :]
        clear(flat, slots)
        rows_t_ref[...] = flat[...].T


def turned(values):
    count, width = values.shape
    full = jnp.concatenate([values, jnp.zeros((LANES - count, width), F32)], axis=0)
    return full.T


def recon_kernel(devices, parts_ref, places_ref, dec_ref, message_ref, live_ref, live, total):
    blocks = dec_ref.shape[0] // STRIDE
    slots = devices * CAP
    step = pl.program_id(0)

    @pl.when(step == 0)
    def _():
        values = jnp.sum(parts_ref[...], axis=0)
        live_ref[...] = values
        live[...] = turned(values)
        total[...] = jnp.zeros(total.shape, F32)

    lane = iota((slots, STRIDE), 1).astype(F32)
    column = iota((slots, LANES), 1)
    pieces = []
    for block in range(blocks):
        here = column == step * blocks + block
        place = jnp.sum(jnp.where(here, places_ref[0:slots, :], 0.0), axis=1, keepdims=True)
        value = jnp.sum(jnp.where(here, live[0:slots, :], 0.0), axis=1, keepdims=True)
        pieces.append(jnp.where(place == lane, value, 0.0).astype(BF16))
    total[...] += dot(jnp.concatenate(pieces, axis=1), dec_ref[...], NN)

    @pl.when(step == pl.num_programs(0) - 1)
    def _():
        for device in range(devices):
            table = total[pl.ds(device * CAP, CAP), :].astype(BF16)
            put_slots(message_ref, device, table, 0)


def error_kernel(group, message_ref, slots_ref, rows_ref, error_ref, sent_ref, back):
    slots = slots_ref[...]
    recon = jnp.zeros(rows_ref.shape, F32)
    for member in range(group):
        for e in range(EXPERTS):
            take_slots(message_ref, e * group + member, back, e * CAP)
        recon = recon + dot(slots, back[...], TN)
    error = (recon - rows_ref[...].astype(F32)).astype(BF16)
    error_ref[...] = error
    sent = dot(slots, error, NN).astype(BF16)
    for device in range(sent_ref.shape[0]):
        e = device // group
        put_slots(sent_ref, device, sent[e * CAP : (e + 1) * CAP], 0)


def latent_kernel(devices, message_ref, places_t_ref, dec_ref, flat_ref, grad_ref):
    blocks = dec_ref.shape[0] // STRIDE
    slots = devices * CAP
    step = pl.program_id(0)

    @pl.when(step == 0)
    def _():
        for device in range(devices):
            take_slots(message_ref, device, flat_ref, device * CAP)
        clear(flat_ref, slots)

    partial = dot(dec_ref[...], flat_ref[...], NT)
    width = flat_ref.shape[0]
    row = iota((STRIDE, width), 0).astype(F32)
    for block in range(blocks):
        index = step * blocks + block
        part = partial[block * STRIDE : (block + 1) * STRIDE, :]
        here = places_t_ref[pl.ds(index, 1), :] == row
        grad_ref[pl.ds(index, 1), :] = jnp.sum(
            jnp.where(here, part, 0.0), axis=0, keepdims=True
        )


def dec_grad_kernel(places_t_ref, live_ref, flat_ref, out_ref):
    blocks = out_ref.shape[0] // STRIDE
    step = pl.program_id(0)
    row = iota((STRIDE, flat_ref.shape[0]), 0).astype(F32)
    for block in range(blocks):
        index = step * blocks + block
        here = places_t_ref[pl.ds(index, 1), :] == row
        activation = jnp.where(here, live_ref[pl.ds(index, 1), :], 0.0).astype(BF16)
        out_ref[block * STRIDE : (block + 1) * STRIDE, :] = dot(activation, flat_ref[...], NN)


def enc_grad_kernel(rows_t_ref, places_ref, mine_ref, other_ref, out_ref, live):
    blocks = out_ref.shape[1] // STRIDE
    step = pl.program_id(0)

    @pl.when(step == 0)
    def _():
        live[...] = turned(mine_ref[...] + other_ref[...])

    shape = (places_ref.shape[0], STRIDE)
    lane = iota(shape, 1).astype(F32)
    column = iota(places_ref.shape, 1)
    for block in range(blocks):
        here = column == step * blocks + block
        place = jnp.sum(jnp.where(here, places_ref[...], 0.0), axis=1, keepdims=True)
        value = jnp.sum(jnp.where(here, live[...], 0.0), axis=1, keepdims=True)
        pre_grad = jnp.where(place == lane, value, 0.0).astype(BF16)
        out_ref[:, block * STRIDE : (block + 1) * STRIDE] = dot(rows_t_ref[...], pre_grad, NN)


def whole(shape):
    return pl.BlockSpec(shape, lambda *_: (0,) * len(shape))


def struct(shape, dtype):
    return jax.ShapeDtypeStruct(shape, dtype)


def cost(flops, moved):
    return pl.CostEstimate(flops=flops, bytes_accessed=moved, transcendentals=0)


def per_device(rows_in, expert_picks, latent_ids, enc_weight, dec_weight):
    row_count, chan = rows_in.shape
    devices = lax.axis_size("expert")
    chans = lax.axis_size("chan")
    group = devices // EXPERTS
    lat = enc_weight.shape[1]
    blocks = lat // STRIDE
    slots = devices * CAP
    padded = up(slots, LANES)
    pieces = chan // LANES
    deep = up((pieces + 1) * CAP, 16)
    thin = up(pieces * CAP, 16)
    tile = min(lat, 2 * STRIDE)
    steps = lat // tile
    matmul = 2 * slots * chan * lat

    def exchange(message):
        return lax.all_to_all(message, "expert", split_axis=0, concat_axis=0, tiled=True)

    slot_table, message = pl.pallas_call(
        functools.partial(dispatch_kernel, group, blocks),
        out_shape=(
            struct((EXPERTS * CAP, row_count), BF16),
            struct((devices, deep, LANES), BF16),
        ),
        compiler_params=PARAMS,
        name="dispatch",
    )(expert_picks.T, latent_ids, rows_in)
    message = exchange(message)
    rows_t, places, places_t, live = pl.pallas_call(
        functools.partial(encode_kernel, devices),
        grid=(steps,),
        in_specs=[whole(message.shape), pl.BlockSpec((chan, tile), lambda i: (0, i))],
        out_specs=(
            whole((chan, padded)),
            whole((padded, LANES)),
            whole((blocks, padded)),
            whole((blocks, padded)),
        ),
        out_shape=(
            struct((chan, padded), BF16),
            struct((padded, LANES), F32),
            struct((blocks, padded), F32),
            struct((blocks, padded), F32),
        ),
        scratch_shapes=[
            pltpu.VMEM((padded, chan), BF16),
            pltpu.VMEM((padded, LANES), F32),
            pltpu.VMEM((padded, LANES), F32),
        ],
        compiler_params=PARAMS,
        cost_estimate=cost(matmul, 2 * chan * lat),
        name="encode",
    )(message, enc_weight)
    parts = lax.all_gather(live, "chan")
    message, live = pl.pallas_call(
        functools.partial(recon_kernel, devices),
        grid=(steps,),
        in_specs=[
            whole(parts.shape),
            whole(places.shape),
            pl.BlockSpec((tile, chan), lambda i: (i, 0)),
        ],
        out_specs=(whole((devices, thin, LANES)), whole((blocks, padded))),
        out_shape=(struct((devices, thin, LANES), BF16), struct((blocks, padded), F32)),
        scratch_shapes=[pltpu.VMEM((padded, LANES), F32), pltpu.VMEM((slots, chan), F32)],
        compiler_params=PARAMS,
        cost_estimate=cost(matmul, 2 * chan * lat),
        name="recon",
    )(parts, places, dec_weight)
    message = exchange(message)
    recon_error, message = pl.pallas_call(
        functools.partial(error_kernel, group),
        out_shape=(struct(rows_in.shape, BF16), struct((devices, thin, LANES), BF16)),
        scratch_shapes=[pltpu.VMEM((EXPERTS * CAP, chan), BF16)],
        compiler_params=PARAMS,
        name="error",
    )(message, slot_table, rows_in)
    message = exchange(message)
    flat_errors, grad = pl.pallas_call(
        functools.partial(latent_kernel, devices),
        grid=(steps,),
        in_specs=[
            whole(message.shape),
            whole(places_t.shape),
            pl.BlockSpec((tile, chan), lambda i: (i, 0)),
        ],
        out_specs=(whole((padded, chan)), whole((blocks, padded))),
        out_shape=(struct((padded, chan), BF16), struct((blocks, padded), F32)),
        compiler_params=PARAMS,
        cost_estimate=cost(matmul, 2 * chan * lat),
        name="latent",
    )(message, places_t, dec_weight)
    swap = [[(i, i ^ bit) for i in range(chans)] for bit in (1, 2)]
    grad = grad + lax.ppermute(grad, "chan", swap[0])
    other = lax.ppermute(grad, "chan", swap[1])
    dec_grad = pl.pallas_call(
        dec_grad_kernel,
        grid=(steps,),
        in_specs=[whole(places_t.shape), whole(live.shape), whole(flat_errors.shape)],
        out_specs=pl.BlockSpec((tile, chan), lambda i: (i, 0)),
        out_shape=struct(dec_weight.shape, F32),
        compiler_params=PARAMS,
        cost_estimate=cost(matmul, 4 * chan * lat),
        name="dec_grad",
    )(places_t, live, flat_errors)
    enc_grad = pl.pallas_call(
        enc_grad_kernel,
        grid=(steps,),
        in_specs=[
            whole(rows_t.shape),
            whole(places.shape),
            whole(grad.shape),
            whole(other.shape),
        ],
        out_specs=pl.BlockSpec((chan, tile), lambda i: (0, i)),
        out_shape=struct(enc_weight.shape, F32),
        scratch_shapes=[pltpu.VMEM((padded, LANES), F32)],
        compiler_params=PARAMS,
        cost_estimate=cost(matmul, 4 * chan * lat),
        name="enc_grad",
    )(rows_t, places, grad, other)
    return (recon_error, enc_grad, dec_grad)


def solution(mesh):
    placed = (
        P("expert", "chan"),
        P("expert", None),
        P("expert", None, None),
        P("chan", "expert"),
        P("expert", "chan"),
    )
    return jax.shard_map(
        per_device,
        mesh=mesh,
        in_specs=placed,
        out_specs=(P("expert", "chan"), P("chan", "expert"), P("expert", "chan")),
        check_vma=False,
    )
```

```python
import functools

import jax
import jax.numpy as jnp
from jax import lax
from jax.experimental import pallas as pl
from jax.experimental.pallas import tpu as pltpu
from jax.sharding import PartitionSpec as P

LAT = 8192
EXPERTS = 4
TOPK = 32
CAP = 18
STRIDE = LAT // TOPK
LANES = 128
F32 = jnp.float32
BF16 = jnp.bfloat16
DEPTH = 6


def up(value, step):
    return -(-value // step) * step


def iota(shape, dim):
    return lax.broadcasted_iota(jnp.int32, shape, dim)


def dot(left, right, dims):
    return lax.dot_general(left, right, (dims, ((), ())), preferred_element_type=F32)


NN = ((1,), (0,))
NT = ((1,), (1,))
TN = ((0,), (0,))


def put_slots(message_ref, table, first):
    for piece in range(table.shape[1] // LANES):
        message_ref[pl.ds((first + piece) * CAP, CAP), :] = table[
            :, piece * LANES : (piece + 1) * LANES
        ]


def take_slots(message_ref, flat_ref, row):
    for piece in range(flat_ref.shape[1] // LANES):
        flat_ref[pl.ds(row, CAP), piece * LANES : (piece + 1) * LANES] = message_ref[
            pl.ds(piece * CAP, CAP), :
        ]


def clear(ref, first, value):
    if first < ref.shape[0]:
        shape = (ref.shape[0] - first, ref.shape[1])
        ref[first:, :] = jnp.full(shape, value, ref.dtype)


def slot_tables(picks_ref, experts):
    rows = picks_ref.shape[1]
    shape = (experts.shape[0], rows)
    place = iota(shape, 0)
    for first in range(CAP, shape[0], CAP):
        place = jnp.where(iota(shape, 0) >= first, iota(shape, 0) - first, place)
    hits = [picks_ref[j : j + 1, :] == experts for j in range(2)]
    member = (hits[0] | hits[1]).astype(BF16)
    earlier = (iota((rows, rows), 0) < iota((rows, rows), 1)).astype(BF16)
    here = dot(member, earlier, NN) == place.astype(F32)
    return [(hit & here).astype(BF16) for hit in hits]


def peer_experts(me, group, devices, rows):
    shape = (devices * CAP, rows)
    number = iota(shape, 0)
    peer = sum((number < CAP * k).astype(jnp.int32) for k in range(1, devices))
    return (peer ^ me) // group


def dispatch_kernel(group, picks_in, ids_in, rows_in, *refs):
    message_refs, (picks_ref, ids_ref, rows_ref, sems) = refs[:-4], refs[-4:]
    load_kernel(picks_in, ids_in, rows_in, picks_ref, ids_ref, rows_ref, sems)
    devices = len(message_refs)
    rows, chan = rows_ref.shape
    me = lax.axis_index("expert")
    chosen = slot_tables(picks_ref, peer_experts(me, group, devices, rows))
    sent = dot(chosen[0] + chosen[1], rows_ref[...], NN).astype(BF16)
    first = iota((rows, TOPK), 1) * STRIDE
    places = sum(
        dot(chosen[j], (ids_ref[:, j, :] - first + 1).astype(BF16), NN) for j in range(2)
    )
    places = (places - 1.0).astype(BF16)
    pieces = chan // LANES
    for peer, message_ref in enumerate(message_refs):
        part = slice(peer * CAP, (peer + 1) * CAP)
        put_slots(message_ref, sent[part], 0)
        message_ref[pl.ds(pieces * CAP, CAP), 0:TOPK] = places[part]


def encode_kernel(group, devices, *refs):
    message_refs, (enc_ref, dec_in, rows_t_ref, places_ref, places_t_ref, live_ref) = (
        refs[:devices],
        refs[devices : devices + 6],
    )
    dec_ref, flat, live, sem = refs[devices + 6 :]
    late = dec_ref.shape[0]
    copy = pltpu.make_async_copy(dec_in.at[pl.ds(dec_in.shape[0] - late, late), :], dec_ref, sem)
    copy.start()
    blocks = enc_ref.shape[1] // STRIDE
    slots = devices * CAP
    low = lax.axis_index("expert") % group * blocks
    pieces = flat.shape[1] // LANES
    clear(places_ref, slots, -1.0)
    clear(live, slots, 0.0)
    clear(flat, slots, 0.0)
    for peer, message_ref in enumerate(message_refs):
        take_slots(message_ref, flat, peer * CAP)
        places_ref[pl.ds(peer * CAP, CAP), :] = message_ref[
            pl.ds(pieces * CAP, CAP), :
        ].astype(F32)
    places_ref[...] = pltpu.roll(places_ref[...], (LANES - low) % LANES, 1)
    places = places_ref[0:slots, :]
    lane = iota((slots, STRIDE), 1).astype(F32)
    column = iota((slots, LANES), 1)
    total = jnp.zeros((slots, LANES), F32)
    for block in range(blocks):
        part = dot(flat[0:slots, :], enc_ref[:, block * STRIDE : (block + 1) * STRIDE], NN)
        here = places[:, block : block + 1] == lane
        value = jnp.sum(jnp.where(here, part, 0.0), axis=1, keepdims=True)
        total = jnp.where(column == block, value, total)
    live[0:slots, :] = total
    live_ref[...] = live[...].T[0:blocks, :]
    places_t_ref[...] = places_ref[...].T[0:blocks, :]
    rows_t_ref[...] = flat[...].T
    copy.wait()


def turned(values):
    count, width = values.shape
    full = jnp.concatenate([values, jnp.zeros((LANES - count, width), F32)], axis=0)
    return full.T


def recon_kernel(devices, parts_ref, places_ref, early_ref, late_ref, *refs):
    message_refs, live_ref, active = refs[:devices], refs[devices], refs[devices + 1]
    slots = devices * CAP
    values = jnp.sum(parts_ref[...], axis=0)
    live_ref[...] = values
    live = turned(values)
    lane = iota((slots, STRIDE), 1).astype(F32)
    for block in range(values.shape[0]):
        here = places_ref[0:slots, block : block + 1] == lane
        value = jnp.where(here, live[0:slots, block : block + 1], 0.0)
        active[:, block * STRIDE : (block + 1) * STRIDE] = value.astype(BF16)
    early = early_ref.shape[0]
    width = 2 * LANES
    for part in range(early_ref.shape[1] // width):
        span = slice(part * width, (part + 1) * width)
        table = dot(active[:, 0:early], early_ref[:, span], NN)
        table = (table + dot(active[:, early:], late_ref[:, span], NN)).astype(BF16)
        for peer in range(devices):
            rows = table[peer * CAP : (peer + 1) * CAP]
            put_slots(message_refs[peer], rows, part * (width // LANES))


def error_kernel(group, devices, *refs):
    back_refs, (picks_ref, rows_ref, error_ref), sent_refs, back = (
        refs[:devices],
        refs[devices : devices + 3],
        refs[devices + 3 : -1],
        refs[-1],
    )
    experts = peer_experts(lax.axis_index("expert"), group, devices, rows_ref.shape[0])
    slots = sum(slot_tables(picks_ref, experts))
    for peer in range(devices):
        take_slots(back_refs[peer], back, peer * CAP)
    recon = dot(slots, back[...], TN)
    error = (recon - rows_ref[...].astype(F32)).astype(BF16)
    error_ref[...] = error
    sent = dot(slots, error, NN).astype(BF16)
    for peer in range(devices):
        put_slots(sent_refs[peer], sent[peer * CAP : (peer + 1) * CAP], 0)


def back_kernel(devices, *refs):
    message_refs, (places_t_ref, live_ref, early_ref, late_ref, grad_ref, out_ref) = (
        refs[:devices],
        refs[devices : devices + 6],
    )
    flat, buffer, sems = refs[devices + 6 :]
    blocks = places_t_ref.shape[0]
    early = early_ref.shape[0] // STRIDE
    depth = buffer.shape[0]
    clear(flat, devices * CAP, 0.0)
    for peer in range(devices):
        take_slots(message_refs[peer], flat, peer * CAP)
    row = iota((STRIDE, flat.shape[0]), 0).astype(F32)

    def copy(index):
        place = out_ref.at[pl.ds(index * STRIDE, STRIDE), :]
        return pltpu.make_async_copy(buffer.at[index % depth], place, sems.at[index % depth])

    for block in range(blocks):
        here = places_t_ref[block : block + 1, :] == row
        active = jnp.where(here, live_ref[block : block + 1, :], 0.0).astype(BF16)
        if block >= depth:
            copy(block - depth).wait()
        buffer[block % depth] = dot(active, flat[...], NN)
        copy(block).start()
        dec_ref, first = (early_ref, block) if block < early else (late_ref, block - early)
        part = dot(dec_ref[first * STRIDE : (first + 1) * STRIDE, :], flat[...], NT)
        grad_ref[block : block + 1, :] = jnp.sum(
            jnp.where(here, part, 0.0), axis=0, keepdims=True
        )
    for block in range(max(0, blocks - depth), blocks):
        copy(block).wait()


def enc_grad_kernel(rows_t_ref, places_ref, parts_ref, out_ref, buffer, sems):
    blocks = out_ref.shape[1] // STRIDE
    depth = buffer.shape[0]
    live = turned(jnp.sum(parts_ref[...], axis=0))
    lane = iota((places_ref.shape[0], STRIDE), 1).astype(F32)

    def copy(index):
        place = out_ref.at[:, pl.ds(index * STRIDE, STRIDE)]
        return pltpu.make_async_copy(buffer.at[index % depth], place, sems.at[index % depth])

    for block in range(blocks):
        here = places_ref[:, block : block + 1] == lane
        pre_grad = jnp.where(here, live[:, block : block + 1], 0.0).astype(BF16)
        if block >= depth:
            copy(block - depth).wait()
        buffer[block % depth] = dot(rows_t_ref[...], pre_grad, NN)
        copy(block).start()
    for block in range(max(0, blocks - depth), blocks):
        copy(block).wait()


def part_of(source_ref, target_ref):
    if source_ref.shape == target_ref.shape:
        return source_ref
    return source_ref.at[pl.ds(0, target_ref.shape[0]), :]


def load_kernel(*refs):
    count = len(refs) // 2
    sems = refs[-1]
    copies = [
        pltpu.make_async_copy(part_of(refs[i], refs[count + i]), refs[count + i], sems.at[i])
        for i in range(count)
    ]
    for copy in copies:
        copy.start()
    for copy in copies:
        copy.wait()


def params(mebibytes):
    return pltpu.CompilerParams(vmem_limit_bytes=mebibytes * 1024 * 1024)


def struct(shape, dtype):
    return jax.ShapeDtypeStruct(shape, dtype)


def cost(flops, moved):
    return pl.CostEstimate(flops=flops, bytes_accessed=moved, transcendentals=0)


def per_device(rows_in, expert_picks, latent_ids, enc_weight, dec_weight):
    row_count, chan = rows_in.shape
    devices = lax.axis_size("expert")
    group = devices // EXPERTS
    lat = enc_weight.shape[1]
    blocks = lat // STRIDE
    slots = devices * CAP
    padded = up(slots, LANES)
    pieces = chan // LANES
    deep = up((pieces + 1) * CAP, 8)
    thin = up(pieces * CAP, 8)
    matmul = 2 * slots * chan * lat

    def exchange(message):
        return lax.all_to_all(message, "expert", split_axis=0, concat_axis=0, tiled=True)

    def trade(messages):
        if devices > 16:
            order = lax.axis_index("expert") ^ lax.rev(lax.iota(jnp.int32, devices), (0,))
            stack = exchange(jnp.stack(messages)[order])[order]
            return [stack[k] for k in range(devices)]
        swaps = [[(i, i ^ k) for i in range(devices)] for k in reversed(range(1, devices))]
        got = [lax.ppermute(sent, "expert", swap) for sent, swap in zip(messages, swaps)]
        return got + [messages[-1]]

    far = pl.BlockSpec(memory_space=pltpu.HBM)
    near = pl.BlockSpec(memory_space=pltpu.VMEM)
    picks = expert_picks.T
    messages = pl.pallas_call(
        functools.partial(dispatch_kernel, group),
        in_specs=[far] * 3,
        out_shape=(struct((deep, LANES), BF16),) * devices,
        scratch_shapes=[
            pltpu.VMEM(picks.shape, picks.dtype),
            pltpu.VMEM(latent_ids.shape, latent_ids.dtype),
            pltpu.VMEM(rows_in.shape, rows_in.dtype),
            pltpu.SemaphoreType.DMA((3,)),
        ],
        name="dispatch",
    )(picks, latent_ids, rows_in)
    messages = trade(messages)
    early = lat // 2
    enc_near, early_dec = pl.pallas_call(
        load_kernel,
        in_specs=[far] * 2,
        out_specs=(near,) * 2,
        out_shape=(pltpu.VMEM(enc_weight.shape, BF16), pltpu.VMEM((early, chan), BF16)),
        scratch_shapes=[pltpu.SemaphoreType.DMA((2,))],
        compiler_params=params(30),
        cost_estimate=cost(0, 3 * chan * lat),
        name="load",
    )(enc_weight, dec_weight)
    rows_t, places, places_t, live, late_dec = pl.pallas_call(
        functools.partial(encode_kernel, group, devices),
        in_specs=[near] * (devices + 1) + [far],
        out_specs=(near,) * 5,
        out_shape=(
            struct((chan, padded), BF16),
            struct((padded, LANES), F32),
            struct((blocks, padded), F32),
            struct((blocks, padded), F32),
            pltpu.VMEM((lat - early, chan), BF16),
        ),
        scratch_shapes=[
            pltpu.VMEM((padded, chan), BF16),
            pltpu.VMEM((padded, LANES), F32),
            pltpu.SemaphoreType.DMA,
        ],
        compiler_params=params(30),
        cost_estimate=cost(matmul, 2 * chan * lat),
        name="encode",
    )(*messages, enc_near, dec_weight)
    parts = lax.all_gather(live, "chan")
    *messages, live = pl.pallas_call(
        functools.partial(recon_kernel, devices),
        in_specs=[near] * 4,
        out_shape=(struct((thin, LANES), BF16),) * devices + (struct((blocks, padded), F32),),
        scratch_shapes=[pltpu.VMEM((slots, lat), BF16)],
        compiler_params=params(12),
        cost_estimate=cost(matmul, 2 * chan * lat),
        name="recon",
    )(parts, places, early_dec, late_dec)
    messages = trade(messages)
    recon_error, *messages = pl.pallas_call(
        functools.partial(error_kernel, group, devices),
        in_specs=[near] * (devices + 2),
        out_shape=(struct(rows_in.shape, BF16),) + (struct((thin, LANES), BF16),) * devices,
        scratch_shapes=[pltpu.VMEM((slots, chan), BF16)],
        compiler_params=params(8),
        name="error",
    )(*messages, picks, rows_in)
    messages = trade(messages)
    grad, dec_grad = pl.pallas_call(
        functools.partial(back_kernel, devices),
        in_specs=[near] * (devices + 4),
        out_specs=(near, far),
        out_shape=(struct((blocks, padded), F32), struct(dec_weight.shape, F32)),
        scratch_shapes=[
            pltpu.VMEM((padded, chan), BF16),
            pltpu.VMEM((DEPTH, STRIDE, chan), F32),
            pltpu.SemaphoreType.DMA((DEPTH,)),
        ],
        compiler_params=params(20),
        cost_estimate=cost(2 * matmul, 4 * chan * lat),
        name="back",
    )(*messages, places_t, live, early_dec, late_dec)
    parts = lax.all_gather(grad, "chan")
    enc_grad = pl.pallas_call(
        enc_grad_kernel,
        in_specs=[near] * 3,
        out_specs=far,
        out_shape=struct(enc_weight.shape, F32),
        scratch_shapes=[
            pltpu.VMEM((DEPTH, chan, STRIDE), F32),
            pltpu.SemaphoreType.DMA((DEPTH,)),
        ],
        compiler_params=params(20),
        cost_estimate=cost(matmul, 4 * chan * lat),
        name="enc_grad",
    )(rows_t, places, parts)
    return (recon_error, enc_grad, dec_grad)


def solution(mesh):
    placed = (
        P("expert", "chan"),
        P("expert", None),
        P("expert", None, None),
        P("chan", "expert"),
        P("expert", "chan"),
    )
    return jax.shard_map(
        per_device,
        mesh=mesh,
        in_specs=placed,
        out_specs=(P("expert", "chan"), P("chan", "expert"), P("expert", "chan")),
        check_vma=False,
    )
```

```python
import functools

import jax
import jax.numpy as jnp
from jax import lax
from jax.experimental import pallas as pl
from jax.experimental.pallas import tpu as pltpu
from jax.sharding import PartitionSpec as P

LAT = 8192
EXPERTS = 4
TOPK = 32
CAP = 18
STRIDE = LAT // TOPK
LANES = 128
F32 = jnp.float32
BF16 = jnp.bfloat16
DEPTH = 6
DISPATCH, LOAD, ENCODE = 57, 30, 30


def up(value, step):
    return -(-value // step) * step


def iota(shape, dim):
    return lax.broadcasted_iota(jnp.int32, shape, dim)


def dot(left, right, dims):
    return lax.dot_general(left, right, (dims, ((), ())), preferred_element_type=F32)


NN = ((1,), (0,))
NT = ((1,), (1,))
TN = ((0,), (0,))


def put_slots(message_ref, table, first):
    for piece in range(table.shape[1] // LANES):
        message_ref[pl.ds((first + piece) * CAP, CAP), :] = table[
            :, piece * LANES : (piece + 1) * LANES
        ]


def take_slots(message_ref, flat_ref, row):
    for piece in range(flat_ref.shape[1] // LANES):
        flat_ref[pl.ds(row, CAP), piece * LANES : (piece + 1) * LANES] = message_ref[
            pl.ds(piece * CAP, CAP), :
        ]


def clear(ref, first, value):
    if first < ref.shape[0]:
        shape = (ref.shape[0] - first, ref.shape[1])
        ref[first:, :] = jnp.full(shape, value, ref.dtype)


def slot_tables(picks_ref, experts):
    rows = picks_ref.shape[1]
    shape = (experts.shape[0], rows)
    place = iota(shape, 0)
    for first in range(CAP, shape[0], CAP):
        place = jnp.where(iota(shape, 0) >= first, iota(shape, 0) - first, place)
    hits = [picks_ref[j : j + 1, :] == experts for j in range(2)]
    member = (hits[0] | hits[1]).astype(BF16)
    earlier = (iota((rows, rows), 0) < iota((rows, rows), 1)).astype(BF16)
    here = dot(member, earlier, NN) == place.astype(F32)
    return [(hit & here).astype(BF16) for hit in hits]


def numbered(count, rows):
    number = iota((count * CAP, rows), 0)
    return sum((number >= CAP * k).astype(jnp.int32) for k in range(1, count))


def fan_experts(group, rows):
    mine = lax.axis_index("expert") // group
    return mine ^ (EXPERTS - 1 - numbered(EXPERTS, rows))


def peer_experts(group, devices, rows):
    return (lax.axis_index("expert") ^ (devices - 1 - numbered(devices, rows))) // group


def load_part(dec_in, dec_ref, first, sem):
    part = dec_in.at[pl.ds(first, dec_ref.shape[0]), :]
    copy = pltpu.make_async_copy(part, dec_ref, sem)
    copy.start()
    return copy


def dispatch_kernel(group, picks_in, ids_in, rows_in, dec_in, *refs):
    message_refs, (dec_ref, picks_ref, ids_ref, rows_ref, sems, sem) = (
        refs[:EXPERTS],
        refs[EXPERTS:],
    )
    starts = [(picks_in, picks_ref), (ids_in, ids_ref), (rows_in, rows_ref)]
    copies = [
        pltpu.make_async_copy(source, target, sems.at[i])
        for i, (source, target) in enumerate(starts)
    ]
    for copy in copies:
        copy.start()
    load = load_part(dec_in, dec_ref, 0, sem)
    for copy in copies:
        copy.wait()
    rows, chan = rows_ref.shape
    chosen = slot_tables(picks_ref, fan_experts(group, rows))
    sent = dot(chosen[0] + chosen[1], rows_ref[...], NN).astype(BF16)
    first = iota((rows, TOPK), 1) * STRIDE
    places = sum(
        dot(chosen[j], (ids_ref[:, j, :] - first + 1).astype(BF16), NN) for j in range(2)
    )
    places = (places - 1.0).astype(BF16)
    pieces = chan // LANES
    for index, message_ref in enumerate(message_refs):
        span = slice(index * CAP, (index + 1) * CAP)
        put_slots(message_ref, sent[span], 0)
        message_ref[pl.ds(pieces * CAP, CAP), 0:TOPK] = places[span]
    load.wait()


def encode_kernel(group, devices, first_row, *refs):
    message_refs, (enc_ref, dec_in, rows_t_ref, places_ref, places_t_ref, live_ref) = (
        refs[:devices],
        refs[devices : devices + 6],
    )
    dec_ref, flat, live, sem = refs[devices + 6 :]
    load = load_part(dec_in, dec_ref, first_row, sem)
    blocks = enc_ref.shape[1] // STRIDE
    slots = devices * CAP
    low = lax.axis_index("expert") % group * blocks
    pieces = flat.shape[1] // LANES
    clear(places_ref, slots, -1.0)
    clear(live, slots, 0.0)
    clear(flat, slots, 0.0)
    for peer, message_ref in enumerate(message_refs):
        take_slots(message_ref, flat, peer * CAP)
        places_ref[pl.ds(peer * CAP, CAP), :] = message_ref[
            pl.ds(pieces * CAP, CAP), :
        ].astype(F32)
    places_ref[...] = pltpu.roll(places_ref[...], (LANES - low) % LANES, 1)
    places = places_ref[0:slots, :]
    lane = iota((slots, STRIDE), 1).astype(F32)
    column = iota((slots, LANES), 1)
    total = jnp.zeros((slots, LANES), F32)
    for block in range(blocks):
        part = dot(flat[0:slots, :], enc_ref[:, block * STRIDE : (block + 1) * STRIDE], NN)
        here = places[:, block : block + 1] == lane
        value = jnp.sum(jnp.where(here, part, 0.0), axis=1, keepdims=True)
        total = jnp.where(column == block, value, total)
    live[0:slots, :] = total
    live_ref[...] = live[...].T[0:blocks, :]
    places_t_ref[...] = places_ref[...].T[0:blocks, :]
    rows_t_ref[...] = flat[...].T
    load.wait()


def turned(values):
    count, width = values.shape
    full = jnp.concatenate([values, jnp.zeros((LANES - count, width), F32)], axis=0)
    return full.T


def recon_kernel(devices, parts_ref, places_ref, early_ref, late_ref, *refs):
    message_refs, live_ref, active = refs[:devices], refs[devices], refs[devices + 1]
    slots = devices * CAP
    values = jnp.sum(parts_ref[...], axis=0)
    live_ref[...] = values
    live = turned(values)
    lane = iota((slots, STRIDE), 1).astype(F32)
    for block in range(values.shape[0]):
        here = places_ref[0:slots, block : block + 1] == lane
        value = jnp.where(here, live[0:slots, block : block + 1], 0.0)
        active[:, block * STRIDE : (block + 1) * STRIDE] = value.astype(BF16)
    early = early_ref.shape[0]
    width = 2 * LANES
    for part in range(early_ref.shape[1] // width):
        span = slice(part * width, (part + 1) * width)
        table = dot(active[:, 0:early], early_ref[:, span], NN)
        table = (table + dot(active[:, early:], late_ref[:, span], NN)).astype(BF16)
        for peer in range(devices):
            rows = table[peer * CAP : (peer + 1) * CAP]
            put_slots(message_refs[peer], rows, part * (width // LANES))


def error_kernel(group, devices, *refs):
    back_refs, (picks_ref, rows_ref, error_ref), sent_refs, back = (
        refs[:devices],
        refs[devices : devices + 3],
        refs[devices + 3 : -1],
        refs[-1],
    )
    rows = rows_ref.shape[0]
    slots = sum(slot_tables(picks_ref, peer_experts(group, devices, rows)))
    for peer in range(devices):
        take_slots(back_refs[peer], back, peer * CAP)
    recon = dot(slots, back[...], TN)
    error = (recon - rows_ref[...].astype(F32)).astype(BF16)
    error_ref[...] = error
    slots = sum(slot_tables(picks_ref, fan_experts(group, rows)))
    sent = dot(slots, error, NN).astype(BF16)
    for index, sent_ref in enumerate(sent_refs):
        put_slots(sent_ref, sent[index * CAP : (index + 1) * CAP], 0)


def back_kernel(devices, *refs):
    message_refs, places_t_ref, live_ref = refs[:devices], refs[devices], refs[devices + 1]
    dec_refs, (grad_ref, out_ref, flat, buffer, sems) = refs[devices + 2 : -5], refs[-5:]
    blocks = places_t_ref.shape[0]
    dec = [(ref, low) for ref in dec_refs for low in range(0, ref.shape[0], STRIDE)]
    depth = buffer.shape[0]
    clear(flat, devices * CAP, 0.0)
    for peer in range(devices):
        take_slots(message_refs[peer], flat, peer * CAP)
    row = iota((STRIDE, flat.shape[0]), 0).astype(F32)

    def copy(index):
        place = out_ref.at[pl.ds(index * STRIDE, STRIDE), :]
        return pltpu.make_async_copy(buffer.at[index % depth], place, sems.at[index % depth])

    for block in range(blocks):
        here = places_t_ref[block : block + 1, :] == row
        active = jnp.where(here, live_ref[block : block + 1, :], 0.0).astype(BF16)
        if block >= depth:
            copy(block - depth).wait()
        buffer[block % depth] = dot(active, flat[...], NN)
        copy(block).start()
        dec_ref, low = dec[block]
        part = dot(dec_ref[low : low + STRIDE, :], flat[...], NT)
        grad_ref[block : block + 1, :] = jnp.sum(
            jnp.where(here, part, 0.0), axis=0, keepdims=True
        )
    for block in range(max(0, blocks - depth), blocks):
        copy(block).wait()


def enc_grad_kernel(rows_t_ref, places_ref, parts_ref, out_ref, buffer, sems):
    blocks = out_ref.shape[1] // STRIDE
    depth = buffer.shape[0]
    live = turned(jnp.sum(parts_ref[...], axis=0))
    lane = iota((places_ref.shape[0], STRIDE), 1).astype(F32)

    def copy(index):
        place = out_ref.at[:, pl.ds(index * STRIDE, STRIDE)]
        return pltpu.make_async_copy(buffer.at[index % depth], place, sems.at[index % depth])

    for block in range(blocks):
        here = places_ref[:, block : block + 1] == lane
        pre_grad = jnp.where(here, live[:, block : block + 1], 0.0).astype(BF16)
        if block >= depth:
            copy(block - depth).wait()
        buffer[block % depth] = dot(rows_t_ref[...], pre_grad, NN)
        copy(block).start()
    for block in range(max(0, blocks - depth), blocks):
        copy(block).wait()


def load_kernel(source_ref, target_ref, sem):
    copy = pltpu.make_async_copy(source_ref, target_ref, sem)
    copy.start()
    copy.wait()


def params(mebibytes):
    return pltpu.CompilerParams(vmem_limit_bytes=mebibytes * 1024 * 1024)


def struct(shape, dtype):
    return jax.ShapeDtypeStruct(shape, dtype)


def cost(flops, moved):
    return pl.CostEstimate(flops=flops, bytes_accessed=moved, transcendentals=0)


def per_device(rows_in, expert_picks, latent_ids, enc_weight, dec_weight):
    row_count, chan = rows_in.shape
    devices = lax.axis_size("expert")
    group = devices // EXPERTS
    lat = enc_weight.shape[1]
    blocks = lat // STRIDE
    slots = devices * CAP
    padded = up(slots, LANES)
    pieces = chan // LANES
    deep = up((pieces + 1) * CAP, 8)
    thin = up(pieces * CAP, 8)
    matmul = 2 * slots * chan * lat

    def exchange(message):
        return lax.all_to_all(message, "expert", split_axis=0, concat_axis=0, tiled=True)

    far_first = lax.axis_index("expert") ^ lax.rev(lax.iota(jnp.int32, devices), (0,))

    def swap(message, k):
        return lax.ppermute(message, "expert", [(i, i ^ k) for i in range(devices)])

    def trade(messages):
        if devices != 8:
            stack = exchange(jnp.stack(messages)[far_first])[far_first]
            return [stack[i] for i in range(devices)]
        return [swap(messages[i], devices - 1 - i) for i in range(devices - 1)] + [messages[-1]]

    def fan_out(messages):
        if devices != 8:
            where = lax.axis_index("expert") // group ^ lax.iota(jnp.int32, devices) // group
            stack = exchange(jnp.stack(messages)[EXPERTS - 1 - where])[far_first]
            return [stack[i] for i in range(devices)]
        far, middle, next_one, own = messages
        got = {6: swap(far, 6), 4: swap(middle, 4), 3: swap(next_one, 3), 2: swap(next_one, 2)}
        got[1] = swap(own, 1)
        got[7] = swap(got[6], 1)
        got[5] = swap(got[4], 1)
        got[0] = own
        return [got[k] for k in reversed(range(devices))]

    far = pl.BlockSpec(memory_space=pltpu.HBM)
    near = pl.BlockSpec(memory_space=pltpu.VMEM)
    picks = expert_picks.T
    early = blocks // 2 * STRIDE
    *messages, early_dec = pl.pallas_call(
        functools.partial(dispatch_kernel, group),
        in_specs=[far] * 4,
        out_shape=(struct((deep, LANES), BF16),) * EXPERTS
        + (pltpu.VMEM((early, chan), BF16),),
        scratch_shapes=[
            pltpu.VMEM(picks.shape, picks.dtype),
            pltpu.VMEM(latent_ids.shape, latent_ids.dtype),
            pltpu.VMEM(rows_in.shape, rows_in.dtype),
            pltpu.SemaphoreType.DMA((3,)),
            pltpu.SemaphoreType.DMA,
        ],
        compiler_params=params(DISPATCH),
        name="dispatch",
    )(picks, latent_ids, rows_in, dec_weight)
    messages = fan_out(messages)
    enc_near = pl.pallas_call(
        load_kernel,
        in_specs=[far],
        out_specs=near,
        out_shape=pltpu.VMEM(enc_weight.shape, BF16),
        scratch_shapes=[pltpu.SemaphoreType.DMA],
        compiler_params=params(LOAD),
        cost_estimate=cost(0, 2 * chan * lat),
        name="load",
    )(enc_weight)
    rows_t, places, places_t, live, late_dec = pl.pallas_call(
        functools.partial(encode_kernel, group, devices, early),
        in_specs=[near] * (devices + 1) + [far],
        out_specs=(near,) * 5,
        out_shape=(
            struct((chan, padded), BF16),
            struct((padded, LANES), F32),
            struct((blocks, padded), F32),
            struct((blocks, padded), F32),
            pltpu.VMEM((lat - early, chan), BF16),
        ),
        scratch_shapes=[
            pltpu.VMEM((padded, chan), BF16),
            pltpu.VMEM((padded, LANES), F32),
            pltpu.SemaphoreType.DMA,
        ],
        compiler_params=params(ENCODE),
        cost_estimate=cost(matmul, 2 * chan * lat),
        name="encode",
    )(*messages, enc_near, dec_weight)
    parts = lax.all_gather(live, "chan")
    *messages, live = pl.pallas_call(
        functools.partial(recon_kernel, devices),
        in_specs=[near] * 4,
        out_shape=(struct((thin, LANES), BF16),) * devices + (struct((blocks, padded), F32),),
        scratch_shapes=[pltpu.VMEM((slots, lat), BF16)],
        compiler_params=params(12),
        cost_estimate=cost(matmul, 2 * chan * lat),
        name="recon",
    )(parts, places, early_dec, late_dec)
    messages = trade(messages)
    recon_error, *messages = pl.pallas_call(
        functools.partial(error_kernel, group, devices),
        in_specs=[near] * (devices + 2),
        out_shape=(struct(rows_in.shape, BF16),) + (struct((thin, LANES), BF16),) * EXPERTS,
        scratch_shapes=[pltpu.VMEM((slots, chan), BF16)],
        compiler_params=params(8),
        name="error",
    )(*messages, picks, rows_in)
    messages = fan_out(messages)
    grad, dec_grad = pl.pallas_call(
        functools.partial(back_kernel, devices),
        in_specs=[near] * (devices + 4),
        out_specs=(near, far),
        out_shape=(struct((blocks, padded), F32), struct(dec_weight.shape, F32)),
        scratch_shapes=[
            pltpu.VMEM((padded, chan), BF16),
            pltpu.VMEM((DEPTH, STRIDE, chan), F32),
            pltpu.SemaphoreType.DMA((DEPTH,)),
        ],
        compiler_params=params(20),
        cost_estimate=cost(2 * matmul, 4 * chan * lat),
        name="back",
    )(*messages, places_t, live, early_dec, late_dec)
    parts = lax.all_gather(grad, "chan")
    enc_grad = pl.pallas_call(
        enc_grad_kernel,
        in_specs=[near] * 3,
        out_specs=far,
        out_shape=struct(enc_weight.shape, F32),
        scratch_shapes=[
            pltpu.VMEM((DEPTH, chan, STRIDE), F32),
            pltpu.SemaphoreType.DMA((DEPTH,)),
        ],
        compiler_params=params(20),
        cost_estimate=cost(matmul, 4 * chan * lat),
        name="enc_grad",
    )(rows_t, places, parts)
    return (recon_error, enc_grad, dec_grad)


def solution(mesh):
    placed = (
        P("expert", "chan"),
        P("expert", None),
        P("expert", None, None),
        P("chan", "expert"),
        P("expert", "chan"),
    )
    return jax.shard_map(
        per_device,
        mesh=mesh,
        in_specs=placed,
        out_specs=(P("expert", "chan"), P("chan", "expert"), P("expert", "chan")),
        check_vma=False,
    )
```

```python
import functools

import jax
import jax.numpy as jnp
from jax import lax
from jax.experimental import pallas as pl
from jax.experimental.pallas import tpu as pltpu
from jax.sharding import PartitionSpec as P

LAT = 8192
EXPERTS = 4
TOPK = 32
CAP = 18
STRIDE = LAT // TOPK
LANES = 128
F32 = jnp.float32
BF16 = jnp.bfloat16
DEPTH = 10
DISPATCH, LOAD, ENCODE = 57, 30, 30


def up(value, step):
    return -(-value // step) * step


def iota(shape, dim):
    return lax.broadcasted_iota(jnp.int32, shape, dim)


def dot(left, right, dims):
    return lax.dot_general(left, right, (dims, ((), ())), preferred_element_type=F32)


NN = ((1,), (0,))
NT = ((1,), (1,))
TN = ((0,), (0,))


def put_slots(message_ref, table, first):
    for piece in range(table.shape[1] // LANES):
        message_ref[pl.ds((first + piece) * CAP, CAP), :] = table[
            :, piece * LANES : (piece + 1) * LANES
        ]


def take_slots(message_ref, flat_ref, row):
    for piece in range(flat_ref.shape[1] // LANES):
        flat_ref[pl.ds(row, CAP), piece * LANES : (piece + 1) * LANES] = message_ref[
            pl.ds(piece * CAP, CAP), :
        ]


def clear(ref, first, value):
    if first < ref.shape[0]:
        shape = (ref.shape[0] - first, ref.shape[1])
        ref[first:, :] = jnp.full(shape, value, ref.dtype)


def slot_tables(picks_ref, experts):
    rows = picks_ref.shape[1]
    shape = (experts.shape[0], rows)
    place = iota(shape, 0)
    for first in range(CAP, shape[0], CAP):
        place = jnp.where(iota(shape, 0) >= first, iota(shape, 0) - first, place)
    hits = [picks_ref[j : j + 1, :] == experts for j in range(2)]
    member = (hits[0] | hits[1]).astype(BF16)
    earlier = (iota((rows, rows), 0) < iota((rows, rows), 1)).astype(BF16)
    here = dot(member, earlier, NN) == place.astype(F32)
    return [(hit & here).astype(BF16) for hit in hits]


def numbered(count, rows):
    number = iota((count * CAP, rows), 0)
    return sum((number >= CAP * k).astype(jnp.int32) for k in range(1, count))


def fan_experts(group, rows):
    mine = lax.axis_index("expert") // group
    return mine ^ (EXPERTS - 1 - numbered(EXPERTS, rows))


def peer_experts(group, devices, rows):
    return (lax.axis_index("expert") ^ (devices - 1 - numbered(devices, rows))) // group


def load_part(dec_in, dec_ref, first, sem):
    part = dec_in.at[pl.ds(first, dec_ref.shape[0]), :]
    copy = pltpu.make_async_copy(part, dec_ref, sem)
    copy.start()
    return copy


def dispatch_kernel(group, picks_in, ids_in, rows_in, dec_in, *refs):
    message_refs, (fan_ref, peer_ref, dec_ref, picks_ref, ids_ref, rows_ref, sems, sem) = (
        refs[:EXPERTS],
        refs[EXPERTS:],
    )
    starts = [(picks_in, picks_ref), (ids_in, ids_ref), (rows_in, rows_ref)]
    copies = [
        pltpu.make_async_copy(source, target, sems.at[i])
        for i, (source, target) in enumerate(starts)
    ]
    for copy in copies:
        copy.start()
    load = load_part(dec_in, dec_ref, 0, sem)
    for copy in copies:
        copy.wait()
    rows, chan = rows_ref.shape
    chosen = slot_tables(picks_ref, fan_experts(group, rows))
    fan_ref[...] = chosen[0] + chosen[1]
    devices = peer_ref.shape[0] // CAP
    peer_ref[...] = sum(slot_tables(picks_ref, peer_experts(group, devices, rows)))
    sent = dot(fan_ref[...], rows_ref[...], NN).astype(BF16)
    first = iota((rows, TOPK), 1) * STRIDE
    places = sum(
        dot(chosen[j], (ids_ref[:, j, :] - first + 1).astype(BF16), NN) for j in range(2)
    )
    places = (places - 1.0).astype(BF16)
    pieces = chan // LANES
    for index, message_ref in enumerate(message_refs):
        span = slice(index * CAP, (index + 1) * CAP)
        put_slots(message_ref, sent[span], 0)
        message_ref[pl.ds(pieces * CAP, CAP), 0:TOPK] = places[span]
    load.wait()


def encode_kernel(group, devices, first_row, *refs):
    message_refs, (enc_ref, dec_in, rows_t_ref, places_ref, places_t_ref, live_ref) = (
        refs[:devices],
        refs[devices : devices + 6],
    )
    dec_ref, flat, live, sem = refs[devices + 6 :]
    load = load_part(dec_in, dec_ref, first_row, sem)
    blocks = enc_ref.shape[1] // STRIDE
    slots = devices * CAP
    low = lax.axis_index("expert") % group * blocks
    pieces = flat.shape[1] // LANES
    clear(places_ref, slots, -1.0)
    clear(live, slots, 0.0)
    clear(flat, slots, 0.0)
    for peer, message_ref in enumerate(message_refs):
        take_slots(message_ref, flat, peer * CAP)
        places_ref[pl.ds(peer * CAP, CAP), :] = message_ref[
            pl.ds(pieces * CAP, CAP), :
        ].astype(F32)
    places_ref[...] = pltpu.roll(places_ref[...], (LANES - low) % LANES, 1)
    places = places_ref[0:slots, :]
    lane = iota((slots, STRIDE), 1).astype(F32)
    column = iota((slots, LANES), 1)
    total = jnp.zeros((slots, LANES), F32)
    for block in range(blocks):
        part = dot(flat[0:slots, :], enc_ref[:, block * STRIDE : (block + 1) * STRIDE], NN)
        here = places[:, block : block + 1] == lane
        value = jnp.sum(jnp.where(here, part, 0.0), axis=1, keepdims=True)
        total = jnp.where(column == block, value, total)
    live[0:slots, :] = total
    live_ref[...] = live[...].T[0:blocks, :]
    places_t_ref[...] = places_ref[...].T[0:blocks, :]
    rows_t_ref[...] = flat[...].T
    load.wait()


def turned(values):
    count, width = values.shape
    full = jnp.concatenate([values, jnp.zeros((LANES - count, width), F32)], axis=0)
    return full.T


def recon_kernel(devices, parts_ref, places_ref, early_ref, late_ref, *refs):
    message_refs, live_ref, active = refs[:devices], refs[devices], refs[devices + 1]
    slots = devices * CAP
    values = jnp.sum(parts_ref[...], axis=0)
    live_ref[...] = values
    live = turned(values)
    lane = iota((slots, STRIDE), 1).astype(F32)
    for block in range(values.shape[0]):
        here = places_ref[0:slots, block : block + 1] == lane
        value = jnp.where(here, live[0:slots, block : block + 1], 0.0)
        active[:, block * STRIDE : (block + 1) * STRIDE] = value.astype(BF16)
    early = early_ref.shape[0]
    width = 2 * LANES
    for part in range(early_ref.shape[1] // width):
        span = slice(part * width, (part + 1) * width)
        table = dot(active[:, 0:early], early_ref[:, span], NN)
        table = (table + dot(active[:, early:], late_ref[:, span], NN)).astype(BF16)
        for peer in range(devices):
            rows = table[peer * CAP : (peer + 1) * CAP]
            put_slots(message_refs[peer], rows, part * (width // LANES))


def error_kernel(devices, *refs):
    back_refs, (fan_ref, peer_ref, rows_ref, error_ref), sent_refs, back = (
        refs[:devices],
        refs[devices : devices + 4],
        refs[devices + 4 : -1],
        refs[-1],
    )
    for peer in range(devices):
        take_slots(back_refs[peer], back, peer * CAP)
    recon = dot(peer_ref[...], back[...], TN)
    error = (recon - rows_ref[...].astype(F32)).astype(BF16)
    error_ref[...] = error
    sent = dot(fan_ref[...], error, NN).astype(BF16)
    for index, sent_ref in enumerate(sent_refs):
        put_slots(sent_ref, sent[index * CAP : (index + 1) * CAP], 0)


def back_kernel(devices, *refs):
    message_refs, places_t_ref, live_ref = refs[:devices], refs[devices], refs[devices + 1]
    dec_refs, (grad_ref, out_ref, flat, buffer, sems) = refs[devices + 2 : -5], refs[-5:]
    blocks = places_t_ref.shape[0]
    dec = [(ref, low) for ref in dec_refs for low in range(0, ref.shape[0], STRIDE)]
    depth = buffer.shape[0]
    clear(flat, devices * CAP, 0.0)
    for peer in range(devices):
        take_slots(message_refs[peer], flat, peer * CAP)
    row = iota((STRIDE, flat.shape[0]), 0).astype(F32)

    def copy(index):
        place = out_ref.at[pl.ds(index * STRIDE, STRIDE), :]
        return pltpu.make_async_copy(buffer.at[index % depth], place, sems.at[index % depth])

    for block in range(blocks):
        here = places_t_ref[block : block + 1, :] == row
        active = jnp.where(here, live_ref[block : block + 1, :], 0.0).astype(BF16)
        if block >= depth:
            copy(block - depth).wait()
        buffer[block % depth] = dot(active, flat[...], NN)
        copy(block).start()
        dec_ref, low = dec[block]
        part = dot(dec_ref[low : low + STRIDE, :], flat[...], NT)
        grad_ref[block : block + 1, :] = jnp.sum(
            jnp.where(here, part, 0.0), axis=0, keepdims=True
        )
    for block in range(max(0, blocks - depth), blocks):
        copy(block).wait()


def enc_grad_kernel(rows_t_ref, places_ref, parts_ref, out_ref, buffer, sems):
    blocks = out_ref.shape[1] // STRIDE
    depth = buffer.shape[0]
    live = turned(jnp.sum(parts_ref[...], axis=0))
    lane = iota((places_ref.shape[0], STRIDE), 1).astype(F32)

    def copy(index):
        place = out_ref.at[:, pl.ds(index * STRIDE, STRIDE)]
        return pltpu.make_async_copy(buffer.at[index % depth], place, sems.at[index % depth])

    for block in range(blocks):
        here = places_ref[:, block : block + 1] == lane
        pre_grad = jnp.where(here, live[:, block : block + 1], 0.0).astype(BF16)
        if block >= depth:
            copy(block - depth).wait()
        buffer[block % depth] = dot(rows_t_ref[...], pre_grad, NN)
        copy(block).start()
    for block in range(max(0, blocks - depth), blocks):
        copy(block).wait()


def load_kernel(source_ref, target_ref, sem):
    copy = pltpu.make_async_copy(source_ref, target_ref, sem)
    copy.start()
    copy.wait()


def params(mebibytes):
    return pltpu.CompilerParams(vmem_limit_bytes=mebibytes * 1024 * 1024)


def struct(shape, dtype):
    return jax.ShapeDtypeStruct(shape, dtype)


def cost(flops, moved):
    return pl.CostEstimate(flops=flops, bytes_accessed=moved, transcendentals=0)


def per_device(rows_in, expert_picks, latent_ids, enc_weight, dec_weight):
    row_count, chan = rows_in.shape
    devices = lax.axis_size("expert")
    group = devices // EXPERTS
    lat = enc_weight.shape[1]
    blocks = lat // STRIDE
    slots = devices * CAP
    padded = up(slots, LANES)
    pieces = chan // LANES
    deep = up((pieces + 1) * CAP, 8)
    thin = up(pieces * CAP, 8)
    matmul = 2 * slots * chan * lat

    def exchange(message):
        return lax.all_to_all(message, "expert", split_axis=0, concat_axis=0, tiled=True)

    far_first = lax.axis_index("expert") ^ lax.rev(lax.iota(jnp.int32, devices), (0,))

    def swap(message, k):
        return lax.ppermute(message, "expert", [(i, i ^ k) for i in range(devices)])

    def trade(messages):
        if devices != 8:
            stack = exchange(jnp.stack(messages)[far_first])[far_first]
            return [stack[i] for i in range(devices)]
        return [swap(messages[i], devices - 1 - i) for i in range(devices - 1)] + [messages[-1]]

    def fan_out(messages):
        if devices != 8:
            where = lax.axis_index("expert") // group ^ lax.iota(jnp.int32, devices) // group
            stack = exchange(jnp.stack(messages)[EXPERTS - 1 - where])[far_first]
            return [stack[i] for i in range(devices)]
        far, middle, next_one, own = messages
        got = {6: swap(far, 6), 4: swap(middle, 4), 3: swap(next_one, 3), 2: swap(next_one, 2)}
        got[1] = swap(own, 1)
        got[7] = swap(got[6], 1)
        got[5] = swap(got[4], 1)
        got[0] = own
        return [got[k] for k in reversed(range(devices))]

    far = pl.BlockSpec(memory_space=pltpu.HBM)
    near = pl.BlockSpec(memory_space=pltpu.VMEM)
    picks = expert_picks.T
    early = max(1, blocks // 4) * STRIDE
    *messages, fan_slots, peer_slots, early_dec = pl.pallas_call(
        functools.partial(dispatch_kernel, group),
        in_specs=[far] * 4,
        out_shape=(pltpu.VMEM((deep, LANES), BF16),) * EXPERTS
        + (
            struct((EXPERTS * CAP, row_count), BF16),
            struct((slots, row_count), BF16),
            pltpu.VMEM((early, chan), BF16),
        ),
        scratch_shapes=[
            pltpu.VMEM(picks.shape, picks.dtype),
            pltpu.VMEM(latent_ids.shape, latent_ids.dtype),
            pltpu.VMEM(rows_in.shape, rows_in.dtype),
            pltpu.SemaphoreType.DMA((3,)),
            pltpu.SemaphoreType.DMA,
        ],
        compiler_params=params(DISPATCH),
        name="dispatch",
    )(picks, latent_ids, rows_in, dec_weight)
    messages = fan_out(messages)
    enc_near = pl.pallas_call(
        load_kernel,
        in_specs=[far],
        out_specs=near,
        out_shape=pltpu.VMEM(enc_weight.shape, BF16),
        scratch_shapes=[pltpu.SemaphoreType.DMA],
        compiler_params=params(LOAD),
        cost_estimate=cost(0, 2 * chan * lat),
        name="load",
    )(enc_weight)
    rows_t, places, places_t, live, late_dec = pl.pallas_call(
        functools.partial(encode_kernel, group, devices, early),
        in_specs=[near] * (devices + 1) + [far],
        out_specs=(near,) * 5,
        out_shape=(
            struct((chan, padded), BF16),
            struct((padded, LANES), F32),
            struct((blocks, padded), F32),
            struct((blocks, padded), F32),
            pltpu.VMEM((lat - early, chan), BF16),
        ),
        scratch_shapes=[
            pltpu.VMEM((padded, chan), BF16),
            pltpu.VMEM((padded, LANES), F32),
            pltpu.SemaphoreType.DMA,
        ],
        compiler_params=params(ENCODE),
        cost_estimate=cost(matmul, 2 * chan * lat),
        name="encode",
    )(*messages, enc_near, dec_weight)
    parts = lax.all_gather(live, "chan")
    *messages, live = pl.pallas_call(
        functools.partial(recon_kernel, devices),
        in_specs=[near] * 4,
        out_shape=(struct((thin, LANES), BF16),) * devices + (struct((blocks, padded), F32),),
        scratch_shapes=[pltpu.VMEM((slots, lat), BF16)],
        compiler_params=params(12),
        cost_estimate=cost(matmul, 2 * chan * lat),
        name="recon",
    )(parts, places, early_dec, late_dec)
    messages = trade(messages)
    recon_error, *messages = pl.pallas_call(
        functools.partial(error_kernel, devices),
        in_specs=[near] * (devices + 3),
        out_shape=(struct(rows_in.shape, BF16),) + (struct((thin, LANES), BF16),) * EXPERTS,
        scratch_shapes=[pltpu.VMEM((slots, chan), BF16)],
        compiler_params=params(8),
        name="error",
    )(*messages, fan_slots, peer_slots, rows_in)
    messages = fan_out(messages)
    grad, dec_grad = pl.pallas_call(
        functools.partial(back_kernel, devices),
        in_specs=[near] * (devices + 4),
        out_specs=(near, far),
        out_shape=(struct((blocks, padded), F32), struct(dec_weight.shape, F32)),
        scratch_shapes=[
            pltpu.VMEM((padded, chan), BF16),
            pltpu.VMEM((DEPTH, STRIDE, chan), F32),
            pltpu.SemaphoreType.DMA((DEPTH,)),
        ],
        compiler_params=params(20),
        cost_estimate=cost(2 * matmul, 4 * chan * lat),
        name="back",
    )(*messages, places_t, live, early_dec, late_dec)
    parts = lax.all_gather(grad, "chan")
    enc_grad = pl.pallas_call(
        enc_grad_kernel,
        in_specs=[near] * 3,
        out_specs=far,
        out_shape=struct(enc_weight.shape, F32),
        scratch_shapes=[
            pltpu.VMEM((DEPTH, chan, STRIDE), F32),
            pltpu.SemaphoreType.DMA((DEPTH,)),
        ],
        compiler_params=params(20),
        cost_estimate=cost(matmul, 4 * chan * lat),
        name="enc_grad",
    )(rows_t, places, parts)
    return (recon_error, enc_grad, dec_grad)


def solution(mesh):
    placed = (
        P("expert", "chan"),
        P("expert", None),
        P("expert", None, None),
        P("chan", "expert"),
        P("expert", "chan"),
    )
    return jax.shard_map(
        per_device,
        mesh=mesh,
        in_specs=placed,
        out_specs=(P("expert", "chan"), P("chan", "expert"), P("expert", "chan")),
        check_vma=False,
    )
```

```python
import functools

import jax
import jax.numpy as jnp
from jax import lax
from jax.experimental import pallas as pl
from jax.experimental.pallas import tpu as pltpu
from jax.sharding import PartitionSpec as P

LAT = 8192
EXPERTS = 4
TOPK = 32
CAP = 18
STRIDE = LAT // TOPK
LANES = 128
F32 = jnp.float32
BF16 = jnp.bfloat16
DEPTH = 10
FIRST = 12
DISPATCH, LOAD, ENCODE = 57, 30, 30


def up(value, step):
    return -(-value // step) * step


def iota(shape, dim):
    return lax.broadcasted_iota(jnp.int32, shape, dim)


def dot(left, right, dims):
    return lax.dot_general(left, right, (dims, ((), ())), preferred_element_type=F32)


NN = ((1,), (0,))
NT = ((1,), (1,))
TN = ((0,), (0,))


def put_slots(message_ref, table, first):
    for piece in range(table.shape[1] // LANES):
        message_ref[pl.ds((first + piece) * CAP, CAP), :] = table[
            :, piece * LANES : (piece + 1) * LANES
        ]


def take_slots(message_ref, flat_ref, row):
    for piece in range(flat_ref.shape[1] // LANES):
        flat_ref[pl.ds(row, CAP), piece * LANES : (piece + 1) * LANES] = message_ref[
            pl.ds(piece * CAP, CAP), :
        ]


def clear(ref, first, value):
    if first < ref.shape[0]:
        shape = (ref.shape[0] - first, ref.shape[1])
        ref[first:, :] = jnp.full(shape, value, ref.dtype)


def slot_tables(picks_ref, experts):
    rows = picks_ref.shape[1]
    shape = (experts.shape[0], rows)
    place = iota(shape, 0)
    for first in range(CAP, shape[0], CAP):
        place = jnp.where(iota(shape, 0) >= first, iota(shape, 0) - first, place)
    hits = [picks_ref[j : j + 1, :] == experts for j in range(2)]
    member = (hits[0] | hits[1]).astype(BF16)
    earlier = (iota((rows, rows), 0) < iota((rows, rows), 1)).astype(BF16)
    here = dot(member, earlier, NN) == place.astype(F32)
    return [(hit & here).astype(BF16) for hit in hits]


def numbered(count, rows):
    number = iota((count * CAP, rows), 0)
    return sum((number >= CAP * k).astype(jnp.int32) for k in range(1, count))


def fan_experts(group, rows):
    mine = lax.axis_index("expert") // group
    return mine ^ (EXPERTS - 1 - numbered(EXPERTS, rows))


def peer_experts(group, devices, rows):
    return (lax.axis_index("expert") ^ (devices - 1 - numbered(devices, rows))) // group


def load_part(dec_in, dec_ref, first, sem):
    part = dec_in.at[pl.ds(first, dec_ref.shape[0]), :]
    copy = pltpu.make_async_copy(part, dec_ref, sem)
    copy.start()
    return copy


def dispatch_kernel(group, picks_in, ids_in, rows_in, dec_in, *refs):
    message_refs, (fan_ref, peer_ref, dec_ref, picks_ref, ids_ref, rows_ref, sems, sem) = (
        refs[:EXPERTS],
        refs[EXPERTS:],
    )
    starts = [(picks_in, picks_ref), (ids_in, ids_ref), (rows_in, rows_ref)]
    copies = [
        pltpu.make_async_copy(source, target, sems.at[i])
        for i, (source, target) in enumerate(starts)
    ]
    for copy in copies:
        copy.start()
    load = load_part(dec_in, dec_ref, 0, sem)
    for copy in copies:
        copy.wait()
    rows, chan = rows_ref.shape
    chosen = slot_tables(picks_ref, fan_experts(group, rows))
    fan_ref[...] = chosen[0] + chosen[1]
    devices = peer_ref.shape[0] // CAP
    peer_ref[...] = sum(slot_tables(picks_ref, peer_experts(group, devices, rows)))
    sent = dot(fan_ref[...], rows_ref[...], NN).astype(BF16)
    first = iota((rows, TOPK), 1) * STRIDE
    places = sum(
        dot(chosen[j], (ids_ref[:, j, :] - first + 1).astype(BF16), NN) for j in range(2)
    )
    places = (places - 1.0).astype(BF16)
    pieces = chan // LANES
    for index, message_ref in enumerate(message_refs):
        span = slice(index * CAP, (index + 1) * CAP)
        put_slots(message_ref, sent[span], 0)
        message_ref[pl.ds(pieces * CAP, CAP), 0:TOPK] = places[span]
    load.wait()


def encode_kernel(group, devices, first_row, *refs):
    message_refs, (enc_ref, dec_in, rows_t_ref, places_ref, places_t_ref, live_ref) = (
        refs[:devices],
        refs[devices : devices + 6],
    )
    dec_ref, flat, live, sem = refs[devices + 6 :]
    load = load_part(dec_in, dec_ref, first_row, sem)
    blocks = enc_ref.shape[1] // STRIDE
    slots = devices * CAP
    low = lax.axis_index("expert") % group * blocks
    pieces = flat.shape[1] // LANES
    clear(places_ref, slots, -1.0)
    clear(live, slots, 0.0)
    clear(flat, slots, 0.0)
    for peer, message_ref in enumerate(message_refs):
        take_slots(message_ref, flat, peer * CAP)
        places_ref[pl.ds(peer * CAP, CAP), :] = message_ref[
            pl.ds(pieces * CAP, CAP), :
        ].astype(F32)
    places_ref[...] = pltpu.roll(places_ref[...], (LANES - low) % LANES, 1)
    places = places_ref[0:slots, :]
    lane = iota((slots, STRIDE), 1).astype(F32)
    column = iota((slots, LANES), 1)
    total = jnp.zeros((slots, LANES), F32)
    for block in range(blocks):
        part = dot(flat[0:slots, :], enc_ref[:, block * STRIDE : (block + 1) * STRIDE], NN)
        here = places[:, block : block + 1] == lane
        value = jnp.sum(jnp.where(here, part, 0.0), axis=1, keepdims=True)
        total = jnp.where(column == block, value, total)
    live[0:slots, :] = total
    live_ref[...] = live[...].T[0:blocks, :]
    places_t_ref[...] = places_ref[...].T[0:blocks, :]
    rows_t_ref[...] = flat[...].T
    load.wait()


def turned(values):
    count, width = values.shape
    full = jnp.concatenate([values, jnp.zeros((LANES - count, width), F32)], axis=0)
    return full.T


def recon_kernel(devices, parts_ref, places_ref, early_ref, late_ref, *refs):
    message_refs, live_ref, active = refs[:devices], refs[devices], refs[devices + 1]
    slots = devices * CAP
    values = jnp.sum(parts_ref[...], axis=0)
    live_ref[...] = values
    live = turned(values)
    lane = iota((slots, STRIDE), 1).astype(F32)
    for block in range(values.shape[0]):
        here = places_ref[0:slots, block : block + 1] == lane
        value = jnp.where(here, live[0:slots, block : block + 1], 0.0)
        active[:, block * STRIDE : (block + 1) * STRIDE] = value.astype(BF16)
    early = early_ref.shape[0]
    width = 2 * LANES
    for part in range(early_ref.shape[1] // width):
        span = slice(part * width, (part + 1) * width)
        table = dot(active[:, 0:early], early_ref[:, span], NN)
        table = (table + dot(active[:, early:], late_ref[:, span], NN)).astype(BF16)
        for peer in range(devices):
            rows = table[peer * CAP : (peer + 1) * CAP]
            put_slots(message_refs[peer], rows, part * (width // LANES))


def error_kernel(devices, *refs):
    back_refs, (fan_ref, peer_ref, rows_ref, error_ref), sent_refs, back = (
        refs[:devices],
        refs[devices : devices + 4],
        refs[devices + 4 : -1],
        refs[-1],
    )
    for peer in range(devices):
        take_slots(back_refs[peer], back, peer * CAP)
    recon = dot(peer_ref[...], back[...], TN)
    error = (recon - rows_ref[...].astype(F32)).astype(BF16)
    error_ref[...] = error
    sent = dot(fan_ref[...], error, NN).astype(BF16)
    for index, sent_ref in enumerate(sent_refs):
        put_slots(sent_ref, sent[index * CAP : (index + 1) * CAP], 0)


def write_dec_grad(places_t_ref, live_ref, flat, out_ref, buffer, sems, blocks, beside):
    depth = buffer.shape[0]
    row = iota((STRIDE, flat.shape[0]), 0).astype(F32)
    copies = []
    for index, block in enumerate(blocks):
        here = places_t_ref[block : block + 1, :] == row
        active = jnp.where(here, live_ref[block : block + 1, :], 0.0).astype(BF16)
        if index >= depth:
            copies[index - depth].wait()
        slot = index % depth
        buffer[slot] = dot(active, flat[...], NN)
        place = out_ref.at[pl.ds(block * STRIDE, STRIDE), :]
        copies.append(pltpu.make_async_copy(buffer.at[slot], place, sems.at[slot]))
        copies[-1].start()
        beside(index)
    for copy in copies[-depth:]:
        copy.wait()


def back_kernel(devices, first, *refs):
    message_refs, places_t_ref, live_ref = refs[:devices], refs[devices], refs[devices + 1]
    dec_refs, (grad_ref, out_ref, flat, buffer, sems) = refs[devices + 2 : -5], refs[-5:]
    blocks = places_t_ref.shape[0]
    dec = [(ref, low) for ref in dec_refs for low in range(0, ref.shape[0], STRIDE)]
    clear(flat, devices * CAP, 0.0)
    for peer in range(devices):
        take_slots(message_refs[peer], flat, peer * CAP)
    row = iota((STRIDE, flat.shape[0]), 0).astype(F32)

    def latents(index):
        for block in range(index * blocks // first, (index + 1) * blocks // first):
            dec_ref, low = dec[block]
            part = dot(dec_ref[low : low + STRIDE, :], flat[...], NT)
            here = places_t_ref[block : block + 1, :] == row
            grad_ref[block : block + 1, :] = jnp.sum(
                jnp.where(here, part, 0.0), axis=0, keepdims=True
            )

    write_dec_grad(
        places_t_ref, live_ref, flat, out_ref, buffer, sems, range(first), latents
    )


def rest_kernel(first, places_t_ref, live_ref, flat, begun_ref, out_ref, buffer, sems):
    blocks = range(first, places_t_ref.shape[0])
    write_dec_grad(
        places_t_ref, live_ref, flat, out_ref, buffer, sems, blocks, lambda index: None
    )


def enc_grad_kernel(rows_t_ref, places_ref, mine_ref, other_ref, out_ref, buffer, sems):
    blocks = out_ref.shape[1] // STRIDE
    depth = buffer.shape[0]
    live = turned(mine_ref[...] + other_ref[...])
    lane = iota((places_ref.shape[0], STRIDE), 1).astype(F32)

    def copy(index):
        place = out_ref.at[:, pl.ds(index * STRIDE, STRIDE)]
        return pltpu.make_async_copy(buffer.at[index % depth], place, sems.at[index % depth])

    for block in range(blocks):
        here = places_ref[:, block : block + 1] == lane
        pre_grad = jnp.where(here, live[:, block : block + 1], 0.0).astype(BF16)
        if block >= depth:
            copy(block - depth).wait()
        buffer[block % depth] = dot(rows_t_ref[...], pre_grad, NN)
        copy(block).start()
    for block in range(max(0, blocks - depth), blocks):
        copy(block).wait()


def load_kernel(source_ref, target_ref, sem):
    copy = pltpu.make_async_copy(source_ref, target_ref, sem)
    copy.start()
    copy.wait()


def params(mebibytes):
    return pltpu.CompilerParams(vmem_limit_bytes=mebibytes * 1024 * 1024)


def struct(shape, dtype):
    return jax.ShapeDtypeStruct(shape, dtype)


def cost(flops, moved):
    return pl.CostEstimate(flops=flops, bytes_accessed=moved, transcendentals=0)


def per_device(rows_in, expert_picks, latent_ids, enc_weight, dec_weight):
    row_count, chan = rows_in.shape
    devices = lax.axis_size("expert")
    chans = lax.axis_size("chan")
    group = devices // EXPERTS
    lat = enc_weight.shape[1]
    blocks = lat // STRIDE
    slots = devices * CAP
    padded = up(slots, LANES)
    pieces = chan // LANES
    deep = up((pieces + 1) * CAP, 8)
    thin = up(pieces * CAP, 8)
    matmul = 2 * slots * chan * lat

    def exchange(message):
        return lax.all_to_all(message, "expert", split_axis=0, concat_axis=0, tiled=True)

    far_first = lax.axis_index("expert") ^ lax.rev(lax.iota(jnp.int32, devices), (0,))

    def swap(message, k):
        return lax.ppermute(message, "expert", [(i, i ^ k) for i in range(devices)])

    def trade(messages):
        if devices != 8:
            stack = exchange(jnp.stack(messages)[far_first])[far_first]
            return [stack[i] for i in range(devices)]
        return [swap(messages[i], devices - 1 - i) for i in range(devices - 1)] + [messages[-1]]

    def fan_out(messages):
        if devices != 8:
            where = lax.axis_index("expert") // group ^ lax.iota(jnp.int32, devices) // group
            stack = exchange(jnp.stack(messages)[EXPERTS - 1 - where])[far_first]
            return [stack[i] for i in range(devices)]
        far, middle, next_one, own = messages
        got = {6: swap(far, 6), 4: swap(middle, 4), 3: swap(next_one, 3), 2: swap(next_one, 2)}
        got[1] = swap(own, 1)
        got[7] = swap(got[6], 1)
        got[5] = swap(got[4], 1)
        got[0] = own
        return [got[k] for k in reversed(range(devices))]

    far = pl.BlockSpec(memory_space=pltpu.HBM)
    near = pl.BlockSpec(memory_space=pltpu.VMEM)
    picks = expert_picks.T
    early = max(1, blocks // 4) * STRIDE
    *messages, fan_slots, peer_slots, early_dec = pl.pallas_call(
        functools.partial(dispatch_kernel, group),
        in_specs=[far] * 4,
        out_shape=(pltpu.VMEM((deep, LANES), BF16),) * EXPERTS
        + (
            struct((EXPERTS * CAP, row_count), BF16),
            struct((slots, row_count), BF16),
            pltpu.VMEM((early, chan), BF16),
        ),
        scratch_shapes=[
            pltpu.VMEM(picks.shape, picks.dtype),
            pltpu.VMEM(latent_ids.shape, latent_ids.dtype),
            pltpu.VMEM(rows_in.shape, rows_in.dtype),
            pltpu.SemaphoreType.DMA((3,)),
            pltpu.SemaphoreType.DMA,
        ],
        compiler_params=params(DISPATCH),
        name="dispatch",
    )(picks, latent_ids, rows_in, dec_weight)
    messages = fan_out(messages)
    enc_near = pl.pallas_call(
        load_kernel,
        in_specs=[far],
        out_specs=near,
        out_shape=pltpu.VMEM(enc_weight.shape, BF16),
        scratch_shapes=[pltpu.SemaphoreType.DMA],
        compiler_params=params(LOAD),
        cost_estimate=cost(0, 2 * chan * lat),
        name="load",
    )(enc_weight)
    rows_t, places, places_t, live, late_dec = pl.pallas_call(
        functools.partial(encode_kernel, group, devices, early),
        in_specs=[near] * (devices + 1) + [far],
        out_specs=(near,) * 5,
        out_shape=(
            struct((chan, padded), BF16),
            struct((padded, LANES), F32),
            struct((blocks, padded), F32),
            struct((blocks, padded), F32),
            pltpu.VMEM((lat - early, chan), BF16),
        ),
        scratch_shapes=[
            pltpu.VMEM((padded, chan), BF16),
            pltpu.VMEM((padded, LANES), F32),
            pltpu.SemaphoreType.DMA,
        ],
        compiler_params=params(ENCODE),
        cost_estimate=cost(matmul, 2 * chan * lat),
        name="encode",
    )(*messages, enc_near, dec_weight)
    parts = lax.all_gather(live, "chan")
    *messages, live = pl.pallas_call(
        functools.partial(recon_kernel, devices),
        in_specs=[near] * 4,
        out_shape=(struct((thin, LANES), BF16),) * devices + (struct((blocks, padded), F32),),
        scratch_shapes=[pltpu.VMEM((slots, lat), BF16)],
        compiler_params=params(12),
        cost_estimate=cost(matmul, 2 * chan * lat),
        name="recon",
    )(parts, places, early_dec, late_dec)
    messages = trade(messages)
    recon_error, *messages = pl.pallas_call(
        functools.partial(error_kernel, devices),
        in_specs=[near] * (devices + 3),
        out_shape=(struct(rows_in.shape, BF16),) + (struct((thin, LANES), BF16),) * EXPERTS,
        scratch_shapes=[pltpu.VMEM((slots, chan), BF16)],
        compiler_params=params(8),
        name="error",
    )(*messages, fan_slots, peer_slots, rows_in)
    messages = fan_out(messages)
    first = max(1, blocks * FIRST // 16)
    grad, dec_grad, flat = pl.pallas_call(
        functools.partial(back_kernel, devices, first),
        in_specs=[near] * (devices + 4),
        out_specs=(near, far, near),
        out_shape=(
            struct((blocks, padded), F32),
            struct(dec_weight.shape, F32),
            struct((padded, chan), BF16),
        ),
        scratch_shapes=[
            pltpu.VMEM((first, STRIDE, chan), F32),
            pltpu.SemaphoreType.DMA((first,)),
        ],
        compiler_params=params(20),
        cost_estimate=cost(2 * matmul, 2 * chan * lat),
        name="back",
    )(*messages, places_t, live, early_dec, late_dec)

    def across(values, bit):
        return lax.ppermute(values, "chan", [(i, i ^ bit) for i in range(chans)])

    bit = 1
    while 2 * bit < chans:
        grad = grad + across(grad, bit)
        bit = 2 * bit
    other = across(grad, bit)
    dec_grad = pl.pallas_call(
        functools.partial(rest_kernel, first),
        in_specs=[near] * 3 + [far],
        out_specs=far,
        out_shape=struct(dec_weight.shape, F32),
        input_output_aliases={3: 0},
        scratch_shapes=[
            pltpu.VMEM((DEPTH, STRIDE, chan), F32),
            pltpu.SemaphoreType.DMA((DEPTH,)),
        ],
        compiler_params=params(20),
        cost_estimate=cost(matmul, 3 * chan * lat),
        name="rest",
    )(places_t, live, flat, dec_grad)
    enc_grad = pl.pallas_call(
        enc_grad_kernel,
        in_specs=[near] * 4,
        out_specs=far,
        out_shape=struct(enc_weight.shape, F32),
        scratch_shapes=[
            pltpu.VMEM((DEPTH, chan, STRIDE), F32),
            pltpu.SemaphoreType.DMA((DEPTH,)),
        ],
        compiler_params=params(20),
        cost_estimate=cost(matmul, 4 * chan * lat),
        name="enc_grad",
    )(rows_t, places, grad, other)
    return (recon_error, enc_grad, dec_grad)


def solution(mesh):
    placed = (
        P("expert", "chan"),
        P("expert", None),
        P("expert", None, None),
        P("chan", "expert"),
        P("expert", "chan"),
    )
    return jax.shard_map(
        per_device,
        mesh=mesh,
        in_specs=placed,
        out_specs=(P("expert", "chan"), P("chan", "expert"), P("expert", "chan")),
        check_vma=False,
    )
```

```python
import functools

import jax
import jax.numpy as jnp
from jax import lax
from jax.experimental import pallas as pl
from jax.experimental.pallas import tpu as pltpu
from jax.sharding import PartitionSpec as P

LAT = 8192
EXPERTS = 4
TOPK = 32
CAP = 18
STRIDE = LAT // TOPK
LANES = 128
F32 = jnp.float32
BF16 = jnp.bfloat16
DEPTH = 10
FIRST = 12
LAST = 40
DISPATCH, LOAD, ENCODE = 57, 30, 30


def up(value, step):
    return -(-value // step) * step


def iota(shape, dim):
    return lax.broadcasted_iota(jnp.int32, shape, dim)


def dot(left, right, dims):
    return lax.dot_general(left, right, (dims, ((), ())), preferred_element_type=F32)


NN = ((1,), (0,))
NT = ((1,), (1,))
TN = ((0,), (0,))


def put_slots(message_ref, table, first):
    for piece in range(table.shape[1] // LANES):
        message_ref[pl.ds((first + piece) * CAP, CAP), :] = table[
            :, piece * LANES : (piece + 1) * LANES
        ]


def take_slots(message_ref, flat_ref, row):
    for piece in range(flat_ref.shape[1] // LANES):
        flat_ref[pl.ds(row, CAP), piece * LANES : (piece + 1) * LANES] = message_ref[
            pl.ds(piece * CAP, CAP), :
        ]


def clear(ref, first, value):
    if first < ref.shape[0]:
        shape = (ref.shape[0] - first, ref.shape[1])
        ref[first:, :] = jnp.full(shape, value, ref.dtype)


def slot_tables(picks_ref, experts):
    rows = picks_ref.shape[1]
    shape = (experts.shape[0], rows)
    place = iota(shape, 0)
    for first in range(CAP, shape[0], CAP):
        place = jnp.where(iota(shape, 0) >= first, iota(shape, 0) - first, place)
    hits = [picks_ref[j : j + 1, :] == experts for j in range(2)]
    member = (hits[0] | hits[1]).astype(BF16)
    earlier = (iota((rows, rows), 0) < iota((rows, rows), 1)).astype(BF16)
    here = dot(member, earlier, NN) == place.astype(F32)
    return [(hit & here).astype(BF16) for hit in hits]


def numbered(count, rows):
    number = iota((count * CAP, rows), 0)
    return sum((number >= CAP * k).astype(jnp.int32) for k in range(1, count))


def fan_experts(group, rows):
    mine = lax.axis_index("expert") // group
    return mine ^ (EXPERTS - 1 - numbered(EXPERTS, rows))


def peer_experts(group, devices, rows):
    return (lax.axis_index("expert") ^ (devices - 1 - numbered(devices, rows))) // group


def load_part(dec_in, dec_ref, first, sem):
    part = dec_in.at[pl.ds(first, dec_ref.shape[0]), :]
    copy = pltpu.make_async_copy(part, dec_ref, sem)
    copy.start()
    return copy


def dispatch_kernel(group, picks_in, ids_in, rows_in, dec_in, *refs):
    message_refs, (fan_ref, peer_ref, dec_ref, picks_ref, ids_ref, rows_ref, sems, sem) = (
        refs[:EXPERTS],
        refs[EXPERTS:],
    )
    starts = [(picks_in, picks_ref), (ids_in, ids_ref), (rows_in, rows_ref)]
    copies = [
        pltpu.make_async_copy(source, target, sems.at[i])
        for i, (source, target) in enumerate(starts)
    ]
    for copy in copies:
        copy.start()
    load = load_part(dec_in, dec_ref, 0, sem)
    for copy in copies:
        copy.wait()
    rows, chan = rows_ref.shape
    chosen = slot_tables(picks_ref, fan_experts(group, rows))
    fan_ref[...] = chosen[0] + chosen[1]
    devices = peer_ref.shape[0] // CAP
    peer_ref[...] = sum(slot_tables(picks_ref, peer_experts(group, devices, rows)))
    sent = dot(fan_ref[...], rows_ref[...], NN).astype(BF16)
    first = iota((rows, TOPK), 1) * STRIDE
    places = sum(
        dot(chosen[j], (ids_ref[:, j, :] - first + 1).astype(BF16), NN) for j in range(2)
    )
    places = (places - 1.0).astype(BF16)
    pieces = chan // LANES
    for index, message_ref in enumerate(message_refs):
        span = slice(index * CAP, (index + 1) * CAP)
        put_slots(message_ref, sent[span], 0)
        message_ref[pl.ds(pieces * CAP, CAP), 0:TOPK] = places[span]
    load.wait()


def encode_kernel(group, devices, first_row, *refs):
    message_refs, (enc_ref, dec_in, rows_t_ref, places_ref, places_t_ref, live_ref) = (
        refs[:devices],
        refs[devices : devices + 6],
    )
    dec_ref, flat, live, sem = refs[devices + 6 :]
    load = load_part(dec_in, dec_ref, first_row, sem)
    blocks = enc_ref.shape[1] // STRIDE
    slots = devices * CAP
    low = lax.axis_index("expert") % group * blocks
    pieces = flat.shape[1] // LANES
    clear(places_ref, slots, -1.0)
    clear(live, slots, 0.0)
    clear(flat, slots, 0.0)
    for peer, message_ref in enumerate(message_refs):
        take_slots(message_ref, flat, peer * CAP)
        places_ref[pl.ds(peer * CAP, CAP), :] = message_ref[
            pl.ds(pieces * CAP, CAP), :
        ].astype(F32)
    places_ref[...] = pltpu.roll(places_ref[...], (LANES - low) % LANES, 1)
    places = places_ref[0:slots, :]
    lane = iota((slots, STRIDE), 1).astype(F32)
    column = iota((slots, LANES), 1)
    total = jnp.zeros((slots, LANES), F32)
    for block in range(blocks):
        part = dot(flat[0:slots, :], enc_ref[:, block * STRIDE : (block + 1) * STRIDE], NN)
        here = places[:, block : block + 1] == lane
        value = jnp.sum(jnp.where(here, part, 0.0), axis=1, keepdims=True)
        total = jnp.where(column == block, value, total)
    live[0:slots, :] = total
    live_ref[...] = live[...].T[0:blocks, :]
    places_t_ref[...] = places_ref[...].T[0:blocks, :]
    rows_t_ref[...] = flat[...].T
    load.wait()


def turned(values):
    count, width = values.shape
    full = jnp.concatenate([values, jnp.zeros((LANES - count, width), F32)], axis=0)
    return full.T


def recon_kernel(devices, count, mine_ref, other_ref, places_ref, *refs):
    dec_refs, refs = refs[:count], refs[count:]
    message_refs, live_ref, active = refs[:devices], refs[devices], refs[devices + 1]
    slots = devices * CAP
    values = mine_ref[...] + other_ref[...]
    live_ref[...] = values
    live = turned(values)
    lane = iota((slots, STRIDE), 1).astype(F32)
    for block in range(values.shape[0]):
        here = places_ref[0:slots, block : block + 1] == lane
        value = jnp.where(here, live[0:slots, block : block + 1], 0.0)
        active[:, block * STRIDE : (block + 1) * STRIDE] = value.astype(BF16)
    width = 2 * LANES
    for part in range(dec_refs[0].shape[1] // width):
        span = slice(part * width, (part + 1) * width)
        low, table = 0, 0.0
        for dec_ref in dec_refs:
            high = low + dec_ref.shape[0]
            table = table + dot(active[:, low:high], dec_ref[:, span], NN)
            low = high
        table = table.astype(BF16)
        for peer in range(devices):
            rows = table[peer * CAP : (peer + 1) * CAP]
            put_slots(message_refs[peer], rows, part * (width // LANES))


def error_kernel(devices, *refs):
    back_refs, (fan_ref, peer_ref, rows_ref, error_ref), sent_refs, back = (
        refs[:devices],
        refs[devices : devices + 4],
        refs[devices + 4 : -1],
        refs[-1],
    )
    for peer in range(devices):
        take_slots(back_refs[peer], back, peer * CAP)
    recon = dot(peer_ref[...], back[...], TN)
    error = (recon - rows_ref[...].astype(F32)).astype(BF16)
    error_ref[...] = error
    sent = dot(fan_ref[...], error, NN).astype(BF16)
    for index, sent_ref in enumerate(sent_refs):
        put_slots(sent_ref, sent[index * CAP : (index + 1) * CAP], 0)


def write_dec_grad(places_t_ref, live_ref, flat, out_ref, buffer, sems, blocks, beside):
    depth = buffer.shape[0]
    row = iota((STRIDE, flat.shape[0]), 0).astype(F32)
    copies = []
    for index, block in enumerate(blocks):
        here = places_t_ref[block : block + 1, :] == row
        active = jnp.where(here, live_ref[block : block + 1, :], 0.0).astype(BF16)
        if index >= depth:
            copies[index - depth].wait()
        slot = index % depth
        buffer[slot] = dot(active, flat[...], NN)
        place = out_ref.at[pl.ds(block * STRIDE, STRIDE), :]
        copies.append(pltpu.make_async_copy(buffer.at[slot], place, sems.at[slot]))
        copies[-1].start()
        beside(index)
    for copy in copies[-depth:]:
        copy.wait()


def back_kernel(devices, first, *refs):
    message_refs, places_t_ref, live_ref = refs[:devices], refs[devices], refs[devices + 1]
    dec_refs, (grad_ref, out_ref, flat, buffer, sems) = refs[devices + 2 : -5], refs[-5:]
    blocks = places_t_ref.shape[0]
    dec = [(ref, low) for ref in dec_refs for low in range(0, ref.shape[0], STRIDE)]
    clear(flat, devices * CAP, 0.0)
    for peer in range(devices):
        take_slots(message_refs[peer], flat, peer * CAP)
    row = iota((STRIDE, flat.shape[0]), 0).astype(F32)

    def latents(index):
        for block in range(index * blocks // first, (index + 1) * blocks // first):
            dec_ref, low = dec[block]
            part = dot(dec_ref[low : low + STRIDE, :], flat[...], NT)
            here = places_t_ref[block : block + 1, :] == row
            grad_ref[block : block + 1, :] = jnp.sum(
                jnp.where(here, part, 0.0), axis=0, keepdims=True
            )

    write_dec_grad(
        places_t_ref, live_ref, flat, out_ref, buffer, sems, range(first), latents
    )


def rest_kernel(first, places_t_ref, live_ref, flat, begun_ref, out_ref, buffer, sems):
    blocks = range(first, places_t_ref.shape[0])
    write_dec_grad(
        places_t_ref, live_ref, flat, out_ref, buffer, sems, blocks, lambda index: None
    )


def enc_grad_kernel(rows_t_ref, places_ref, mine_ref, other_ref, out_ref, buffer, sems):
    blocks = out_ref.shape[1] // STRIDE
    depth = buffer.shape[0]
    live = turned(mine_ref[...] + other_ref[...])
    lane = iota((places_ref.shape[0], STRIDE), 1).astype(F32)

    def copy(index):
        place = out_ref.at[:, pl.ds(index * STRIDE, STRIDE)]
        return pltpu.make_async_copy(buffer.at[index % depth], place, sems.at[index % depth])

    for block in range(blocks):
        here = places_ref[:, block : block + 1] == lane
        pre_grad = jnp.where(here, live[:, block : block + 1], 0.0).astype(BF16)
        if block >= depth:
            copy(block - depth).wait()
        buffer[block % depth] = dot(rows_t_ref[...], pre_grad, NN)
        copy(block).start()
    for block in range(max(0, blocks - depth), blocks):
        copy(block).wait()


def load_kernel(first, source_ref, target_ref, sem):
    load_part(source_ref, target_ref, first, sem).wait()


def params(mebibytes):
    return pltpu.CompilerParams(vmem_limit_bytes=mebibytes * 1024 * 1024)


def struct(shape, dtype):
    return jax.ShapeDtypeStruct(shape, dtype)


def cost(flops, moved):
    return pl.CostEstimate(flops=flops, bytes_accessed=moved, transcendentals=0)


def per_device(rows_in, expert_picks, latent_ids, enc_weight, dec_weight):
    row_count, chan = rows_in.shape
    devices = lax.axis_size("expert")
    chans = lax.axis_size("chan")
    group = devices // EXPERTS
    lat = enc_weight.shape[1]
    blocks = lat // STRIDE
    slots = devices * CAP
    padded = up(slots, LANES)
    pieces = chan // LANES
    deep = up((pieces + 1) * CAP, 8)
    thin = up(pieces * CAP, 8)
    matmul = 2 * slots * chan * lat

    def exchange(message):
        return lax.all_to_all(message, "expert", split_axis=0, concat_axis=0, tiled=True)

    far_first = lax.axis_index("expert") ^ lax.rev(lax.iota(jnp.int32, devices), (0,))

    def swap(message, k):
        return lax.ppermute(message, "expert", [(i, i ^ k) for i in range(devices)])

    def trade(messages):
        if devices != 8:
            stack = exchange(jnp.stack(messages)[far_first])[far_first]
            return [stack[i] for i in range(devices)]
        return [swap(messages[i], devices - 1 - i) for i in range(devices - 1)] + [messages[-1]]

    def fan_out(messages):
        if devices != 8:
            where = lax.axis_index("expert") // group ^ lax.iota(jnp.int32, devices) // group
            stack = exchange(jnp.stack(messages)[EXPERTS - 1 - where])[far_first]
            return [stack[i] for i in range(devices)]
        far, middle, next_one, own = messages
        got = {6: swap(far, 6), 4: swap(middle, 4), 3: swap(next_one, 3), 2: swap(next_one, 2)}
        got[1] = swap(own, 1)
        got[7] = swap(got[6], 1)
        got[5] = swap(got[4], 1)
        got[0] = own
        return [got[k] for k in reversed(range(devices))]

    far = pl.BlockSpec(memory_space=pltpu.HBM)
    near = pl.BlockSpec(memory_space=pltpu.VMEM)
    picks = expert_picks.T
    early = max(1, blocks // 4) * STRIDE
    middle = -(-(lat - early) // (2 * STRIDE)) * STRIDE
    last = lat - early - middle
    *messages, fan_slots, peer_slots, early_dec = pl.pallas_call(
        functools.partial(dispatch_kernel, group),
        in_specs=[far] * 4,
        out_shape=(pltpu.VMEM((deep, LANES), BF16),) * EXPERTS
        + (
            struct((EXPERTS * CAP, row_count), BF16),
            struct((slots, row_count), BF16),
            pltpu.VMEM((early, chan), BF16),
        ),
        scratch_shapes=[
            pltpu.VMEM(picks.shape, picks.dtype),
            pltpu.VMEM(latent_ids.shape, latent_ids.dtype),
            pltpu.VMEM(rows_in.shape, rows_in.dtype),
            pltpu.SemaphoreType.DMA((3,)),
            pltpu.SemaphoreType.DMA,
        ],
        compiler_params=params(DISPATCH),
        name="dispatch",
    )(picks, latent_ids, rows_in, dec_weight)
    messages = fan_out(messages)
    enc_near = pl.pallas_call(
        functools.partial(load_kernel, 0),
        in_specs=[far],
        out_specs=near,
        out_shape=pltpu.VMEM(enc_weight.shape, BF16),
        scratch_shapes=[pltpu.SemaphoreType.DMA],
        compiler_params=params(LOAD),
        cost_estimate=cost(0, 2 * chan * lat),
        name="load",
    )(enc_weight)
    rows_t, places, places_t, live, middle_dec = pl.pallas_call(
        functools.partial(encode_kernel, group, devices, early),
        in_specs=[near] * (devices + 1) + [far],
        out_specs=(near,) * 5,
        out_shape=(
            struct((chan, padded), BF16),
            struct((padded, LANES), F32),
            struct((blocks, padded), F32),
            struct((blocks, padded), F32),
            pltpu.VMEM((middle, chan), BF16),
        ),
        scratch_shapes=[
            pltpu.VMEM((padded, chan), BF16),
            pltpu.VMEM((padded, LANES), F32),
            pltpu.SemaphoreType.DMA,
        ],
        compiler_params=params(ENCODE),
        cost_estimate=cost(matmul, 2 * chan * lat),
        name="encode",
    )(*messages, enc_near, dec_weight)
    def across(values, bit):
        return lax.ppermute(values, "chan", [(i, i ^ bit) for i in range(chans)])

    def pair(values):
        bit = 1
        while 2 * bit < chans:
            values = values + across(values, bit)
            bit = 2 * bit
        return values, across(values, bit)

    mine, other = pair(live)
    dec_parts = [early_dec, middle_dec]
    if last:
        last_dec = pl.pallas_call(
            functools.partial(load_kernel, early + middle),
            in_specs=[far],
            out_specs=near,
            out_shape=pltpu.VMEM((last, chan), BF16),
            scratch_shapes=[pltpu.SemaphoreType.DMA],
            compiler_params=params(LAST),
            cost_estimate=cost(0, 2 * chan * last),
            name="load_last",
        )(dec_weight)
        dec_parts.append(last_dec)
    *messages, live = pl.pallas_call(
        functools.partial(recon_kernel, devices, len(dec_parts)),
        in_specs=[near] * (3 + len(dec_parts)),
        out_shape=(struct((thin, LANES), BF16),) * devices + (struct((blocks, padded), F32),),
        scratch_shapes=[pltpu.VMEM((slots, lat), BF16)],
        compiler_params=params(12),
        cost_estimate=cost(matmul, 2 * chan * lat),
        name="recon",
    )(mine, other, places, *dec_parts)
    messages = trade(messages)
    recon_error, *messages = pl.pallas_call(
        functools.partial(error_kernel, devices),
        in_specs=[near] * (devices + 3),
        out_shape=(struct(rows_in.shape, BF16),) + (struct((thin, LANES), BF16),) * EXPERTS,
        scratch_shapes=[pltpu.VMEM((slots, chan), BF16)],
        compiler_params=params(8),
        name="error",
    )(*messages, fan_slots, peer_slots, rows_in)
    messages = fan_out(messages)
    first = max(1, blocks * FIRST // 16)
    grad, dec_grad, flat = pl.pallas_call(
        functools.partial(back_kernel, devices, first),
        in_specs=[near] * (devices + 2 + len(dec_parts)),
        out_specs=(near, far, near),
        out_shape=(
            struct((blocks, padded), F32),
            struct(dec_weight.shape, F32),
            struct((padded, chan), BF16),
        ),
        scratch_shapes=[
            pltpu.VMEM((first, STRIDE, chan), F32),
            pltpu.SemaphoreType.DMA((first,)),
        ],
        compiler_params=params(20),
        cost_estimate=cost(2 * matmul, 2 * chan * lat),
        name="back",
    )(*messages, places_t, live, *dec_parts)

    grad, other = pair(grad)
    dec_grad = pl.pallas_call(
        functools.partial(rest_kernel, first),
        in_specs=[near] * 3 + [far],
        out_specs=far,
        out_shape=struct(dec_weight.shape, F32),
        input_output_aliases={3: 0},
        scratch_shapes=[
            pltpu.VMEM((DEPTH, STRIDE, chan), F32),
            pltpu.SemaphoreType.DMA((DEPTH,)),
        ],
        compiler_params=params(20),
        cost_estimate=cost(matmul, 3 * chan * lat),
        name="rest",
    )(places_t, live, flat, dec_grad)
    enc_grad = pl.pallas_call(
        enc_grad_kernel,
        in_specs=[near] * 4,
        out_specs=far,
        out_shape=struct(enc_weight.shape, F32),
        scratch_shapes=[
            pltpu.VMEM((DEPTH, chan, STRIDE), F32),
            pltpu.SemaphoreType.DMA((DEPTH,)),
        ],
        compiler_params=params(20),
        cost_estimate=cost(matmul, 4 * chan * lat),
        name="enc_grad",
    )(rows_t, places, grad, other)
    return (recon_error, enc_grad, dec_grad)


def solution(mesh):
    placed = (
        P("expert", "chan"),
        P("expert", None),
        P("expert", None, None),
        P("chan", "expert"),
        P("expert", "chan"),
    )
    return jax.shard_map(
        per_device,
        mesh=mesh,
        in_specs=placed,
        out_specs=(P("expert", "chan"), P("chan", "expert"), P("expert", "chan")),
        check_vma=False,
    )
```

```python
import functools

import jax
import jax.numpy as jnp
from jax import lax
from jax.experimental import pallas as pl
from jax.experimental.pallas import tpu as pltpu
from jax.sharding import PartitionSpec as P

LAT = 8192
EXPERTS = 4
TOPK = 32
CAP = 18
STRIDE = LAT // TOPK
LANES = 128
F32 = jnp.float32
BF16 = jnp.bfloat16
DEPTH = 10
FIRST = 12
LOADS = 4
LAST = 40
DISPATCH, LOAD, ENCODE = 57, 30, 30


def up(value, step):
    return -(-value // step) * step


def iota(shape, dim):
    return lax.broadcasted_iota(jnp.int32, shape, dim)


def dot(left, right, dims):
    return lax.dot_general(left, right, (dims, ((), ())), preferred_element_type=F32)


NN = ((1,), (0,))
NT = ((1,), (1,))
TN = ((0,), (0,))


def put_slots(message_ref, table, first):
    for piece in range(table.shape[1] // LANES):
        message_ref[pl.ds((first + piece) * CAP, CAP), :] = table[
            :, piece * LANES : (piece + 1) * LANES
        ]


def take_slots(message_ref, flat_ref, row):
    for piece in range(flat_ref.shape[1] // LANES):
        flat_ref[pl.ds(row, CAP), piece * LANES : (piece + 1) * LANES] = message_ref[
            pl.ds(piece * CAP, CAP), :
        ]


def clear(ref, first, value):
    if first < ref.shape[0]:
        shape = (ref.shape[0] - first, ref.shape[1])
        ref[first:, :] = jnp.full(shape, value, ref.dtype)


def slot_tables(picks_ref, experts):
    rows = picks_ref.shape[1]
    shape = (experts.shape[0], rows)
    place = iota(shape, 0)
    for first in range(CAP, shape[0], CAP):
        place = jnp.where(iota(shape, 0) >= first, iota(shape, 0) - first, place)
    hits = [picks_ref[j : j + 1, :] == experts for j in range(2)]
    member = (hits[0] | hits[1]).astype(BF16)
    earlier = (iota((rows, rows), 0) < iota((rows, rows), 1)).astype(BF16)
    here = dot(member, earlier, NN) == place.astype(F32)
    return [(hit & here).astype(BF16) for hit in hits]


def numbered(count, rows):
    number = iota((count * CAP, rows), 0)
    return sum((number >= CAP * k).astype(jnp.int32) for k in range(1, count))


def fan_experts(group, rows):
    mine = lax.axis_index("expert") // group
    return mine ^ (EXPERTS - 1 - numbered(EXPERTS, rows))


def peer_experts(group, devices, rows):
    return (lax.axis_index("expert") ^ (devices - 1 - numbered(devices, rows))) // group


def load_part(dec_in, dec_ref, first, sem):
    part = dec_in.at[pl.ds(first, dec_ref.shape[0]), :]
    copy = pltpu.make_async_copy(part, dec_ref, sem)
    copy.start()
    return copy


def dispatch_kernel(group, picks_in, ids_in, rows_in, dec_in, *refs):
    message_refs, (fan_ref, peer_ref, dec_ref, picks_ref, ids_ref, rows_ref, sems, sem) = (
        refs[:EXPERTS],
        refs[EXPERTS:],
    )
    starts = [(picks_in, picks_ref), (ids_in, ids_ref), (rows_in, rows_ref)]
    copies = [
        pltpu.make_async_copy(source, target, sems.at[i])
        for i, (source, target) in enumerate(starts)
    ]
    for copy in copies:
        copy.start()
    load = load_part(dec_in, dec_ref, 0, sem)
    for copy in copies:
        copy.wait()
    rows, chan = rows_ref.shape
    chosen = slot_tables(picks_ref, fan_experts(group, rows))
    fan_ref[...] = chosen[0] + chosen[1]
    devices = peer_ref.shape[0] // CAP
    peer_ref[...] = sum(slot_tables(picks_ref, peer_experts(group, devices, rows)))
    sent = dot(fan_ref[...], rows_ref[...], NN).astype(BF16)
    first = iota((rows, TOPK), 1) * STRIDE
    places = sum(
        dot(chosen[j], (ids_ref[:, j, :] - first + 1).astype(BF16), NN) for j in range(2)
    )
    places = (places - 1.0).astype(BF16)
    pieces = chan // LANES
    for index, message_ref in enumerate(message_refs):
        span = slice(index * CAP, (index + 1) * CAP)
        put_slots(message_ref, sent[span], 0)
        message_ref[pl.ds(pieces * CAP, CAP), 0:TOPK] = places[span]
    load.wait()


def encode_kernel(group, devices, first_row, *refs):
    message_refs, (enc_ref, dec_in, rows_t_ref, places_ref, places_t_ref, live_ref) = (
        refs[:devices],
        refs[devices : devices + 6],
    )
    dec_ref, flat, live, sem = refs[devices + 6 :]
    load = load_part(dec_in, dec_ref, first_row, sem)
    blocks = enc_ref.shape[1] // STRIDE
    slots = devices * CAP
    low = lax.axis_index("expert") % group * blocks
    pieces = flat.shape[1] // LANES
    clear(places_ref, slots, -1.0)
    clear(live, slots, 0.0)
    clear(flat, slots, 0.0)
    for peer, message_ref in enumerate(message_refs):
        take_slots(message_ref, flat, peer * CAP)
        places_ref[pl.ds(peer * CAP, CAP), :] = message_ref[
            pl.ds(pieces * CAP, CAP), :
        ].astype(F32)
    places_ref[...] = pltpu.roll(places_ref[...], (LANES - low) % LANES, 1)
    places = places_ref[0:slots, :]
    lane = iota((slots, STRIDE), 1).astype(F32)
    column = iota((slots, LANES), 1)
    total = jnp.zeros((slots, LANES), F32)
    for block in range(blocks):
        part = dot(flat[0:slots, :], enc_ref[:, block * STRIDE : (block + 1) * STRIDE], NN)
        here = places[:, block : block + 1] == lane
        value = jnp.sum(jnp.where(here, part, 0.0), axis=1, keepdims=True)
        total = jnp.where(column == block, value, total)
    live[0:slots, :] = total
    live_ref[...] = live[...].T[0:blocks, :]
    places_t_ref[...] = places_ref[...].T[0:blocks, :]
    rows_t_ref[...] = flat[...].T
    load.wait()


def turned(values):
    count, width = values.shape
    full = jnp.concatenate([values, jnp.zeros((LANES - count, width), F32)], axis=0)
    return full.T


def recon_kernel(devices, count, mine_ref, other_ref, places_ref, *refs):
    dec_refs, refs = refs[:count], refs[count:]
    message_refs, live_ref, active = refs[:devices], refs[devices], refs[devices + 1]
    slots = devices * CAP
    values = mine_ref[...] + other_ref[...]
    live_ref[...] = values
    live = turned(values)
    lane = iota((slots, STRIDE), 1).astype(F32)
    for block in range(values.shape[0]):
        here = places_ref[0:slots, block : block + 1] == lane
        value = jnp.where(here, live[0:slots, block : block + 1], 0.0)
        active[:, block * STRIDE : (block + 1) * STRIDE] = value.astype(BF16)
    width = 2 * LANES
    for part in range(dec_refs[0].shape[1] // width):
        span = slice(part * width, (part + 1) * width)
        low, table = 0, 0.0
        for dec_ref in dec_refs:
            high = low + dec_ref.shape[0]
            table = table + dot(active[:, low:high], dec_ref[:, span], NN)
            low = high
        table = table.astype(BF16)
        for peer in range(devices):
            rows = table[peer * CAP : (peer + 1) * CAP]
            put_slots(message_refs[peer], rows, part * (width // LANES))


def error_kernel(devices, *refs):
    back_refs, (fan_ref, peer_ref, rows_ref, error_ref), sent_refs, back = (
        refs[:devices],
        refs[devices : devices + 4],
        refs[devices + 4 : -1],
        refs[-1],
    )
    for peer in range(devices):
        take_slots(back_refs[peer], back, peer * CAP)
    recon = dot(peer_ref[...], back[...], TN)
    error = (recon - rows_ref[...].astype(F32)).astype(BF16)
    error_ref[...] = error
    sent = dot(fan_ref[...], error, NN).astype(BF16)
    for index, sent_ref in enumerate(sent_refs):
        put_slots(sent_ref, sent[index * CAP : (index + 1) * CAP], 0)


def write_dec_grad(places_t_ref, live_ref, flat, out_ref, buffer, sems, blocks, beside):
    depth = buffer.shape[0]
    row = iota((STRIDE, flat.shape[0]), 0).astype(F32)
    copies = []
    for index, block in enumerate(blocks):
        here = places_t_ref[block : block + 1, :] == row
        active = jnp.where(here, live_ref[block : block + 1, :], 0.0).astype(BF16)
        if index >= depth:
            copies[index - depth].wait()
        slot = index % depth
        buffer[slot] = dot(active, flat[...], NN)
        place = out_ref.at[pl.ds(block * STRIDE, STRIDE), :]
        copies.append(pltpu.make_async_copy(buffer.at[slot], place, sems.at[slot]))
        copies[-1].start()
        beside(index)
    for copy in copies[-depth:]:
        copy.wait()


def back_kernel(devices, first, *refs):
    message_refs, places_t_ref, live_ref = refs[:devices], refs[devices], refs[devices + 1]
    dec_refs, (grad_ref, out_ref, flat, buffer, sems) = refs[devices + 2 : -5], refs[-5:]
    blocks = places_t_ref.shape[0]
    dec = [(ref, low) for ref in dec_refs for low in range(0, ref.shape[0], STRIDE)]
    clear(flat, devices * CAP, 0.0)
    for peer in range(devices):
        take_slots(message_refs[peer], flat, peer * CAP)
    row = iota((STRIDE, flat.shape[0]), 0).astype(F32)

    def latents(index):
        for block in range(index * blocks // first, (index + 1) * blocks // first):
            dec_ref, low = dec[block]
            part = dot(dec_ref[low : low + STRIDE, :], flat[...], NT)
            here = places_t_ref[block : block + 1, :] == row
            grad_ref[block : block + 1, :] = jnp.sum(
                jnp.where(here, part, 0.0), axis=0, keepdims=True
            )

    write_dec_grad(
        places_t_ref, live_ref, flat, out_ref, buffer, sems, range(first), latents
    )


def rest_kernel(first, places_t_ref, live_ref, flat, begun_ref, out_ref, buffer, sems):
    blocks = range(first, places_t_ref.shape[0])
    write_dec_grad(
        places_t_ref, live_ref, flat, out_ref, buffer, sems, blocks, lambda index: None
    )


def enc_grad_kernel(rows_t_ref, places_ref, mine_ref, other_ref, out_ref, buffer, sems):
    blocks = out_ref.shape[1] // STRIDE
    depth = buffer.shape[0]
    live = turned(mine_ref[...] + other_ref[...])
    lane = iota((places_ref.shape[0], STRIDE), 1).astype(F32)

    def copy(index):
        place = out_ref.at[:, pl.ds(index * STRIDE, STRIDE)]
        return pltpu.make_async_copy(buffer.at[index % depth], place, sems.at[index % depth])

    for block in range(blocks):
        here = places_ref[:, block : block + 1] == lane
        pre_grad = jnp.where(here, live[:, block : block + 1], 0.0).astype(BF16)
        if block >= depth:
            copy(block - depth).wait()
        buffer[block % depth] = dot(rows_t_ref[...], pre_grad, NN)
        copy(block).start()
    for block in range(max(0, blocks - depth), blocks):
        copy(block).wait()


def load_kernel(first, source_ref, target_ref, sems):
    rows = target_ref.shape[0] // LOADS
    copies = [
        load_part(source_ref, target_ref.at[pl.ds(i * rows, rows), :], first + i * rows, sems.at[i])
        for i in range(LOADS)
    ]
    for copy in copies:
        copy.wait()


def params(mebibytes):
    return pltpu.CompilerParams(vmem_limit_bytes=mebibytes * 1024 * 1024)


def struct(shape, dtype):
    return jax.ShapeDtypeStruct(shape, dtype)


def cost(flops, moved):
    return pl.CostEstimate(flops=flops, bytes_accessed=moved, transcendentals=0)


def per_device(rows_in, expert_picks, latent_ids, enc_weight, dec_weight):
    row_count, chan = rows_in.shape
    devices = lax.axis_size("expert")
    chans = lax.axis_size("chan")
    group = devices // EXPERTS
    lat = enc_weight.shape[1]
    blocks = lat // STRIDE
    slots = devices * CAP
    padded = up(slots, LANES)
    pieces = chan // LANES
    deep = up((pieces + 1) * CAP, 8)
    thin = up(pieces * CAP, 8)
    matmul = 2 * slots * chan * lat

    def exchange(message):
        return lax.all_to_all(message, "expert", split_axis=0, concat_axis=0, tiled=True)

    far_first = lax.axis_index("expert") ^ lax.rev(lax.iota(jnp.int32, devices), (0,))

    def swap(message, k):
        return lax.ppermute(message, "expert", [(i, i ^ k) for i in range(devices)])

    def trade(messages):
        if devices != 8:
            stack = exchange(jnp.stack(messages)[far_first])[far_first]
            return [stack[i] for i in range(devices)]
        return [swap(messages[i], devices - 1 - i) for i in range(devices - 1)] + [messages[-1]]

    def fan_out(messages):
        if devices != 8:
            where = lax.axis_index("expert") // group ^ lax.iota(jnp.int32, devices) // group
            stack = exchange(jnp.stack(messages)[EXPERTS - 1 - where])[far_first]
            return [stack[i] for i in range(devices)]
        far, middle, next_one, own = messages
        got = {6: swap(far, 6), 4: swap(middle, 4), 3: swap(next_one, 3), 2: swap(next_one, 2)}
        got[1] = swap(own, 1)
        got[7] = swap(got[6], 1)
        got[5] = swap(got[4], 1)
        got[0] = own
        return [got[k] for k in reversed(range(devices))]

    far = pl.BlockSpec(memory_space=pltpu.HBM)
    near = pl.BlockSpec(memory_space=pltpu.VMEM)
    picks = expert_picks.T
    early = max(1, blocks // 4) * STRIDE
    middle = -(-(lat - early) // (2 * STRIDE)) * STRIDE
    last = lat - early - middle
    *messages, fan_slots, peer_slots, early_dec = pl.pallas_call(
        functools.partial(dispatch_kernel, group),
        in_specs=[far] * 4,
        out_shape=(pltpu.VMEM((deep, LANES), BF16),) * EXPERTS
        + (
            struct((EXPERTS * CAP, row_count), BF16),
            struct((slots, row_count), BF16),
            pltpu.VMEM((early, chan), BF16),
        ),
        scratch_shapes=[
            pltpu.VMEM(picks.shape, picks.dtype),
            pltpu.VMEM(latent_ids.shape, latent_ids.dtype),
            pltpu.VMEM(rows_in.shape, rows_in.dtype),
            pltpu.SemaphoreType.DMA((3,)),
            pltpu.SemaphoreType.DMA,
        ],
        compiler_params=params(DISPATCH),
        name="dispatch",
    )(picks, latent_ids, rows_in, dec_weight)
    messages = fan_out(messages)
    enc_near = pl.pallas_call(
        functools.partial(load_kernel, 0),
        in_specs=[far],
        out_specs=near,
        out_shape=pltpu.VMEM(enc_weight.shape, BF16),
        scratch_shapes=[pltpu.SemaphoreType.DMA((LOADS,))],
        compiler_params=params(LOAD),
        cost_estimate=cost(0, 2 * chan * lat),
        name="load",
    )(enc_weight)
    rows_t, places, places_t, live, middle_dec = pl.pallas_call(
        functools.partial(encode_kernel, group, devices, early),
        in_specs=[near] * (devices + 1) + [far],
        out_specs=(near,) * 5,
        out_shape=(
            struct((chan, padded), BF16),
            struct((padded, LANES), F32),
            struct((blocks, padded), F32),
            struct((blocks, padded), F32),
            pltpu.VMEM((middle, chan), BF16),
        ),
        scratch_shapes=[
            pltpu.VMEM((padded, chan), BF16),
            pltpu.VMEM((padded, LANES), F32),
            pltpu.SemaphoreType.DMA,
        ],
        compiler_params=params(ENCODE),
        cost_estimate=cost(matmul, 2 * chan * lat),
        name="encode",
    )(*messages, enc_near, dec_weight)
    def across(values, bit):
        return lax.ppermute(values, "chan", [(i, i ^ bit) for i in range(chans)])

    def pair(values):
        bit = 1
        while 2 * bit < chans:
            values = values + across(values, bit)
            bit = 2 * bit
        return values, across(values, bit)

    mine, other = pair(live)
    dec_parts = [early_dec, middle_dec]
    if last:
        last_dec = pl.pallas_call(
            functools.partial(load_kernel, early + middle),
            in_specs=[far],
            out_specs=near,
            out_shape=pltpu.VMEM((last, chan), BF16),
            scratch_shapes=[pltpu.SemaphoreType.DMA((LOADS,))],
            compiler_params=params(LAST),
            cost_estimate=cost(0, 2 * chan * last),
            name="load_last",
        )(dec_weight)
        dec_parts.append(last_dec)
    *messages, live = pl.pallas_call(
        functools.partial(recon_kernel, devices, len(dec_parts)),
        in_specs=[near] * (3 + len(dec_parts)),
        out_shape=(struct((thin, LANES), BF16),) * devices + (struct((blocks, padded), F32),),
        scratch_shapes=[pltpu.VMEM((slots, lat), BF16)],
        compiler_params=params(12),
        cost_estimate=cost(matmul, 2 * chan * lat),
        name="recon",
    )(mine, other, places, *dec_parts)
    messages = trade(messages)
    recon_error, *messages = pl.pallas_call(
        functools.partial(error_kernel, devices),
        in_specs=[near] * (devices + 3),
        out_shape=(struct(rows_in.shape, BF16),) + (struct((thin, LANES), BF16),) * EXPERTS,
        scratch_shapes=[pltpu.VMEM((slots, chan), BF16)],
        compiler_params=params(8),
        name="error",
    )(*messages, fan_slots, peer_slots, rows_in)
    messages = fan_out(messages)
    first = max(1, blocks * FIRST // 16)
    grad, dec_grad, flat = pl.pallas_call(
        functools.partial(back_kernel, devices, first),
        in_specs=[near] * (devices + 2 + len(dec_parts)),
        out_specs=(near, far, near),
        out_shape=(
            struct((blocks, padded), F32),
            struct(dec_weight.shape, F32),
            struct((padded, chan), BF16),
        ),
        scratch_shapes=[
            pltpu.VMEM((first, STRIDE, chan), F32),
            pltpu.SemaphoreType.DMA((first,)),
        ],
        compiler_params=params(20),
        cost_estimate=cost(2 * matmul, 2 * chan * lat),
        name="back",
    )(*messages, places_t, live, *dec_parts)

    grad, other = pair(grad)
    dec_grad = pl.pallas_call(
        functools.partial(rest_kernel, first),
        in_specs=[near] * 3 + [far],
        out_specs=far,
        out_shape=struct(dec_weight.shape, F32),
        input_output_aliases={3: 0},
        scratch_shapes=[
            pltpu.VMEM((DEPTH, STRIDE, chan), F32),
            pltpu.SemaphoreType.DMA((DEPTH,)),
        ],
        compiler_params=params(20),
        cost_estimate=cost(matmul, 3 * chan * lat),
        name="rest",
    )(places_t, live, flat, dec_grad)
    enc_grad = pl.pallas_call(
        enc_grad_kernel,
        in_specs=[near] * 4,
        out_specs=far,
        out_shape=struct(enc_weight.shape, F32),
        scratch_shapes=[
            pltpu.VMEM((DEPTH, chan, STRIDE), F32),
            pltpu.SemaphoreType.DMA((DEPTH,)),
        ],
        compiler_params=params(20),
        cost_estimate=cost(matmul, 4 * chan * lat),
        name="enc_grad",
    )(rows_t, places, grad, other)
    return (recon_error, enc_grad, dec_grad)


def solution(mesh):
    placed = (
        P("expert", "chan"),
        P("expert", None),
        P("expert", None, None),
        P("chan", "expert"),
        P("expert", "chan"),
    )
    return jax.shard_map(
        per_device,
        mesh=mesh,
        in_specs=placed,
        out_specs=(P("expert", "chan"), P("chan", "expert"), P("expert", "chan")),
        check_vma=False,
    )
```
